128 devices in a mesh: lat: 4 (over y_lo, core), lon: 32 (over z, x, y_hi).
Axes of the slice: x: 4, y: 4 (y_hi: 2, y_lo: 2; y = y_hi * 2 + y_lo), z: 4, core: 2. Of those that a mesh axis runs over, the one named last changes fastest.
Arguments:
- losses: float32 [8, 64, 512, 256], P('lat', 'lon'), may hold values from -6 to 6
- positions: float32 [8, 64, 2, 512], P('lat', 'lon'), may hold values from 0 to 1
- leaf_basis: float32 [8, 64, 512, 64], P('lat', 'lon'), may hold values from -0.25 to 0.25
- near_flags: int32 [8, 64, 9], P('lat', 'lon'), may hold values from 0 to 1, as said below
- leaf_coupling: bfloat16 [8, 64, 36, 64, 64], P('lat', 'lon'), may hold values from -0.75 to 0.75
- leaf_transfer: float32 [8, 64, 64, 64], P('lat', 'lon'), may hold values from -0.75 to 0.75
- device_coupling: bfloat16 [4, 32, 36, 64, 64], P('lat', 'lon'), may hold values from -0.1875 to 0.1875
- device_transfer: float32 [4, 32, 64, 64], replicated, may hold values from -0.75 to 0.75
- group_coupling: bfloat16 [2, 16, 2, 16, 64, 64], replicated, may hold values from -0.09375 to 0.09375
Outputs:
- applied: float32 [8, 64, 512, 256], P('lat', 'lon')
The draws below stay inside these ranges and needn't reach their ends.
Inputs may be any that keep to these rules, and one draw needn't show every extreme that they name: near_flags[i, j, 3 (di + 1) + dj + 1] is 1 when leaf (i + di, (j + dj) mod 64) forms a dense block with leaf (i, j); the flags of a pair agree seen from both leaves, the middle flag is always 1, and flags toward latitude indices outside the grid are 0.
All inputs are finite; a program needn't handle non-finite values.
Results may differ from the reference program's by a relative error of at most 0.0003.
Values sent between devices are 32-bit elements; how exact they have to be, the bound alone decides.
A program may use at most 192 MiB of HBM per device.

```python
import jax
import jax.numpy as jnp
import numpy as np
from jax import lax

LEAF_PTS = 512
RANK = 64
COLS = 256
LEAF_LAT = 2
LEAF_LON = 2
LAT_LEAVES = 8
LON_LEAVES = 64
WINDOW = 36
GROUP_LAT = 2
GROUP_LON = 16
N_LAT = 4
N_LON = 32


def draw_near_flags(key, part):
    density = jax.random.randint(jax.random.fold_in(key, 11), (LAT_LEAVES, LON_LEAVES), 0, 4) * jax.random.randint(jax.random.fold_in(key, 31), (LAT_LEAVES, LON_LEAVES), 0, 2)
    pair_level = jax.random.randint(jax.random.fold_in(key, 23), (LAT_LEAVES, LON_LEAVES, 4), 0, 4)
    forward = ((0, 1), (1, -1), (1, 0), (1, 1))
    row_ids = jnp.arange(LAT_LEAVES, dtype=jnp.int32)
    flag_list = []
    for row_step in (-1, 0, 1):
        for col_step in (-1, 0, 1):
            if row_step == 0 and col_step == 0:
                flag_list.append(jnp.ones((LAT_LEAVES, LON_LEAVES), jnp.int32))
                continue
            other = jnp.roll(density, (-row_step, -col_step), (0, 1))
            if (row_step, col_step) in forward:
                level = pair_level[:, :, forward.index((row_step, col_step))]
            else:
                level = jnp.roll(pair_level[:, :, forward.index((-row_step, -col_step))], (-row_step, -col_step), (0, 1))
            inside = (row_ids + row_step >= 0) & (row_ids + row_step < LAT_LEAVES)
            dense_pair = (jnp.maximum(density, other) > level) & inside[:, None]
            flag_list.append(jnp.where(dense_pair, 1, 0).astype(jnp.int32))
    return jnp.stack(flag_list, -1)


def block_levels(rng, shape, pieces, low, high):
    def one(position, shards_of):
        steps = jax.random.uniform(jax.random.fold_in(jax.random.fold_in(rng, 6), position), (shards_of,), jnp.float32, low / len(pieces), high / len(pieces))
        return jnp.repeat(jnp.exp(steps), shape[position] // shards_of).reshape((-1,) + (1,) * (len(shape) - position - 1))

    loudness = one(*pieces[0])
    for cut in pieces[1:]:
        loudness = loudness * one(*cut)
    return loudness


def scatter_about(own_key, extent, scale, most, shards=(), held_as=jnp.bfloat16):
    gain = block_levels(own_key, extent, shards, -0.22, 0.18) if shards else 1.0
    drawn = jax.random.normal(own_key, extent, jnp.float32) * scale * gain
    return jnp.minimum(jnp.maximum(drawn, -most), most).astype(held_as)


def setup_inputs(seed: int = 0) -> dict:
    streams_of = jax.random.split(jax.random.key(seed), 10)
    return {
        "losses": scatter_about(streams_of[0], (LAT_LEAVES, LON_LEAVES, LEAF_PTS, COLS), 1.0, 6.0, ((0, 4), (1, 32)), jnp.float32),
        "positions": jnp.clip(1.0 * jax.random.uniform(streams_of[1], (LAT_LEAVES, LON_LEAVES, 2, LEAF_PTS), jnp.float32) ** block_levels(streams_of[1], (LAT_LEAVES, LON_LEAVES, 2, LEAF_PTS), ((0, 4), (1, 32)), -0.2, 0.2), 0.0, 1.0),
        "leaf_basis": scatter_about(streams_of[2], (LAT_LEAVES, LON_LEAVES, LEAF_PTS, RANK), LEAF_PTS ** -0.5, 0.25, ((0, 4), (1, 32)), jnp.float32),
        "near_flags": draw_near_flags(jax.random.fold_in(streams_of[9], 71), 0),
        "leaf_coupling": scatter_about(streams_of[4], (LAT_LEAVES, LON_LEAVES, WINDOW, RANK, RANK), RANK ** -0.5, 0.75, ((0, 4), (1, 32))),
        "leaf_transfer": scatter_about(streams_of[5], (LAT_LEAVES, LON_LEAVES, RANK, RANK), RANK ** -0.5, 0.75, ((0, 4), (1, 32)), jnp.float32),
        "device_coupling": scatter_about(streams_of[6], (N_LAT, N_LON, 36, RANK, RANK), (RANK * 16) ** -0.5, 0.1875, ((0, 4), (1, 32))),
        "device_transfer": scatter_about(streams_of[7], (N_LAT, N_LON, RANK, RANK), RANK ** -0.5, 0.75, (), jnp.float32),
        "group_coupling": scatter_about(streams_of[8], (GROUP_LAT, GROUP_LON, GROUP_LAT, GROUP_LON, RANK, RANK), (RANK * 64) ** -0.5, 0.09375),
    }


highest = lax.Precision.HIGHEST
length_scale = 0.15
nugget = 0.5
root_three = 1.7320508075688772

def matern(target, source, row_shift, col_shift):
    delta_row = target[0][:, None] - (source[0][None, :] + row_shift)
    delta_col = target[1][:, None] - (source[1][None, :] + col_shift)
    scaled = root_three / length_scale * jnp.sqrt(delta_row * delta_row + delta_col * delta_col)
    return (1.0 + scaled) * jnp.exp(-scaled)

def zone_table(rows_lat, rows_lon):
    one_hot = np.zeros((rows_lat, rows_lon, 9, 3 * rows_lat, 3 * rows_lon), np.float32)
    for row_leaf in range(rows_lat):
        for col_leaf in range(rows_lon):
            for row_step in range(3):
                for col_step in range(3):
                    one_hot[row_leaf, col_leaf, row_step * 3 + col_step, rows_lat + row_leaf + row_step - 1, rows_lon + col_leaf + col_step - 1] = 1.0
    return one_hot

def group_far(own_row, own_col, group_rows, group_cols):
    rows_far = jnp.abs(jnp.arange(group_rows, dtype=jnp.int32) - own_row) >= 2
    distance = (jnp.arange(group_cols, dtype=jnp.int32) - own_col) % group_cols
    cols_far = (distance >= 2) & (distance <= group_cols - 2)
    return jnp.where(rows_far[:, None] | cols_far[None, :], 1.0, 0.0).astype(jnp.float32)

def device_keep(lat_pos, lon_pos):
    step_ids = jnp.arange(6, dtype=jnp.int32)
    row_ids = 2 * (lat_pos // 2) - 2 + step_ids
    offsets = 2 * (lon_pos // 2) - 2 + step_ids - lon_pos
    inside = (jnp.abs(row_ids - lat_pos) <= 1)[:, None] & (jnp.abs(offsets) <= 1)[None, :]
    return jnp.where(inside, 0.0, 1.0).astype(jnp.float32).reshape(36)

def reference(losses, positions, leaf_basis, near_flags, leaf_coupling, leaf_transfer, device_coupling, device_transfer, group_coupling):
    flags_float = near_flags.astype(jnp.float32)
    loss_pad = jnp.pad(losses, ((1, 1), (0, 0), (0, 0), (0, 0)))
    place_pad = jnp.pad(positions, ((1, 1), (0, 0), (0, 0), (0, 0)))
    leaf_ids = jnp.arange(LAT_LEAVES * LON_LEAVES, dtype=jnp.int32)

    def near_leaf(leaf_index):
        row_leaf = leaf_index // LON_LEAVES
        col_leaf = leaf_index % LON_LEAVES
        own_place = positions[row_leaf, col_leaf]
        near_sum = nugget * losses[row_leaf, col_leaf]
        for row_step in (-1, 0, 1):
            for col_step in (-1, 0, 1):
                flag_value = near_flags[row_leaf, col_leaf, (row_step + 1) * 3 + col_step + 1]
                other_row = row_leaf + row_step + 1
                other_col = (col_leaf + col_step) % LON_LEAVES

                def dense_block(other_row=other_row, other_col=other_col, row_step=row_step, col_step=col_step):
                    kernel = matern(own_place, place_pad[other_row, other_col], float(row_step), float(col_step))
                    return jnp.dot(kernel, loss_pad[other_row, other_col], precision=highest)
                near_sum = near_sum + lax.cond(flag_value > 0, dense_block, lambda: jnp.zeros_like(losses[0, 0]))
        return near_sum
    near = lax.map(near_leaf, leaf_ids).reshape(LAT_LEAVES, LON_LEAVES, LEAF_PTS, COLS)
    leaf_coef = jnp.einsum('ijpr,ijpc->ijrc', leaf_basis, losses, precision=highest)
    coef_pad = jnp.pad(leaf_coef, ((LEAF_LAT, LEAF_LAT), (0, 0), (0, 0), (0, 0)))
    zone_mask = jnp.asarray(zone_table(LEAF_LAT, LEAF_LON)).astype(jnp.float32)

    def leaf_far_one(leaf_index):
        row_leaf = leaf_index // LON_LEAVES
        col_leaf = leaf_index % LON_LEAVES
        lat_pos = row_leaf // LEAF_LAT
        lon_pos = col_leaf // LEAF_LON
        lat_band = lax.dynamic_slice_in_dim(coef_pad, (lat_pos * LEAF_LAT).astype(jnp.int32), 3 * LEAF_LAT, 0)
        columns = ((LEAF_LON * (lon_pos - 1) + jnp.arange(3 * LEAF_LON, dtype=jnp.int32)) % LON_LEAVES).astype(jnp.int32)
        window = jnp.take(lat_band, columns, axis=1).reshape(WINDOW, RANK, COLS)
        covered = jnp.einsum('o,ouv->uv', flags_float[row_leaf, col_leaf], zone_mask[row_leaf % LEAF_LAT, col_leaf % LEAF_LON])
        keep_mask = (1.0 - covered).reshape(WINDOW)
        weights = leaf_coupling[row_leaf, col_leaf].astype(jnp.float32) * keep_mask[:, None, None]
        return jnp.einsum('wrk,wkc->rc', weights, window, precision=highest)
    leaf_far = lax.map(leaf_far_one, leaf_ids).reshape(LAT_LEAVES, LON_LEAVES, RANK, COLS)
    device_coef = jnp.einsum('pbqdkr,pbqdkc->pqrc', leaf_transfer.reshape(N_LAT, LEAF_LAT, N_LON, LEAF_LON, RANK, RANK), leaf_coef.reshape(N_LAT, LEAF_LAT, N_LON, LEAF_LON, RANK, COLS), precision=highest)
    device_pad = jnp.pad(device_coef, ((2, 2), (0, 0), (0, 0), (0, 0)))

    def device_far_one(device_index):
        lat_pos = device_index // N_LON
        lon_pos = device_index % N_LON
        lat_band = lax.dynamic_slice_in_dim(device_pad, (2 * (lat_pos // 2)).astype(jnp.int32), 6, 0)
        columns = ((2 * (lon_pos // 2) - 2 + jnp.arange(6, dtype=jnp.int32)) % N_LON).astype(jnp.int32)
        window = jnp.take(lat_band, columns, axis=1).reshape(36, RANK, COLS)
        weights = device_coupling[lat_pos, lon_pos].astype(jnp.float32) * device_keep(lat_pos, lon_pos)[:, None, None]
        return jnp.einsum('vrk,vkc->rc', weights, window, precision=highest)
    device_far = lax.map(device_far_one, jnp.arange(N_LAT * N_LON, dtype=jnp.int32)).reshape(N_LAT, N_LON, RANK, COLS)
    shares = jnp.einsum('pqkr,pqkc->pqrc', device_transfer, device_coef, precision=highest)
    group_coef = shares.reshape(N_LAT // 2, 2, N_LON // 2, 2, RANK, COLS).sum(axis=(1, 3))

    def group_one(group_index):
        own_row = group_index // (N_LON // 2)
        own_col = group_index % (N_LON // 2)
        far_mask = group_far(own_row, own_col, N_LAT // 2, N_LON // 2)
        weights = group_coupling[own_row, own_col].astype(jnp.float32) * far_mask[:, :, None, None]
        return jnp.einsum('xyrk,xykc->rc', weights, group_coef, precision=highest)
    group_field = lax.map(group_one, jnp.arange(N_LAT // 2 * (N_LON // 2), dtype=jnp.int32)).reshape(N_LAT // 2, N_LON // 2, RANK, COLS)
    spread = jnp.repeat(jnp.repeat(group_field, 2, axis=0), 2, axis=1)
    device_field = device_far + jnp.einsum('pqrk,pqkc->pqrc', device_transfer, spread, precision=highest)
    device_spread = jnp.repeat(jnp.repeat(device_field, LEAF_LAT, axis=0), LEAF_LON, axis=1)
    leaf_field = leaf_far + jnp.einsum('ijrk,ijkc->ijrc', leaf_transfer, device_spread, precision=highest)
    return near + jnp.einsum('ijpr,ijrc->ijpc', leaf_basis, leaf_field, precision=highest)
```

```python
import jax
import jax.numpy as jnp
from jax import lax
from jax.experimental import pallas as pl
from jax.experimental.pallas import tpu as pltpu
from jax.sharding import PartitionSpec as P

MESH = pl.DeviceIdType.MESH
LN2 = 0.6931471805599453
UNIT = 1.7320508075688772 / 0.15 / LN2
AWAY = 1.0e4
f32, bf16 = jnp.float32, jnp.bfloat16


def split(x):
    high = x.astype(bf16)
    return high, (x - high.astype(f32)).astype(bf16)


def mm(a, b, dims=((1,), (0,))):
    return lax.dot_general(a, b, (dims, ((), ())), preferred_element_type=f32)


def mm3(a, b, dims=((1,), (0,))):
    ah, al = split(a)
    bh, bl = split(b)
    return mm(ah, bh, dims) + mm(al, bh, dims) + mm(ah, bl, dims)


def mm2(a, b):
    bh, bl = split(b)
    return mm(a, bh) + mm(a, bl)


LOCAL = ("ext0", "ext1", "ext2", "ext3", "basis", "lcoup", "ltrans", "dcoup", "dtrans", "gcoup", "pext")
FAR = tuple(range(2, 15))
COLUMN = tuple((i, j) for i in range(4) for j in range(2) if (i, j) != (0, 0))


def remote_names():
    names = []
    for kind in ("loss", "place"):
        for which in ("lonp1", "lonp2", "lonm1", "lonm2", "part0", "part1", "cross0", "cross1", "xcp", "xcm", "fwd0", "fwd1"):
            names.append((kind, which))
    for which in ("lonp", "lonm", "part", "cross", "xcp", "xcm", "fwd0", "fwd1"):
        names.append(("coef", which))
    for pair in COLUMN:
        names.append(("cell", pair))
    names += [("win", "p"), ("win", "m")]
    for m in FAR:
        names.append(("group", m))
    return {name: k for k, name in enumerate(names)}


SEMS = remote_names()


def kernel(
    loss_h, place_h, column_ref, flags, basis_h, lcoup_h, ltrans_h, dcoup_h, dtrans_h, gcoup_h,
    out_h,
    ext, pext, coef, cellw, group, gall, acc, kh, kl, sh, sl, field,
    basis, lcoup, ltrans, dcoup, dtrans, gcoup,
    lsem, osem, ssem, rsem,
):
    lat, lon = lax.axis_index("lat"), lax.axis_index("lon")
    n_lon = lax.axis_size("lon")
    par, hi = lax.rem(lat, 2), lax.rem(lon, 2)
    row_group, col_group = lat // 2, lon // 2
    sign = 1 - 2 * par
    has_cross = (lat == 1) | (lat == 2)
    partner, cross = lat + sign, lat - sign

    def leaf(rho, col):
        return 2 * (par + (rho - 1) * sign) + (col - 1)

    def at_lon(step):
        return lax.rem(lon + step + n_lon, n_lon)

    def local(src, dst, k):
        return pltpu.make_async_copy(src, dst, lsem.at[k])

    own_slots = [(1, 1), (1, 2), (2, 1), (2, 2)]
    copies = {}
    for k, (rho, col) in enumerate(own_slots):
        copies[f"ext{k}"] = local(loss_h.at[leaf(rho, col)], ext.at[4 * rho + col], k)
    for k, (src, dst, name) in enumerate((
        (basis_h, basis, "basis"), (lcoup_h, lcoup, "lcoup"), (ltrans_h, ltrans, "ltrans"),
        (dcoup_h, dcoup, "dcoup"), (dtrans_h.at[:, pl.ds(2 * col_group, 2)], dtrans, "dtrans"),
        (gcoup_h.at[row_group, col_group], gcoup, "gcoup"),
    )):
        copies[name] = local(src, dst, 4 + k)
    place_copies = [
        local(place_h.at[leaf(rho, col)], pext.at[4 * rho + col], 10 + k) for k, (rho, col) in enumerate(own_slots)
    ]
    for k in range(4):
        copies[f"ext{k}"].start()
    for name in ("basis", "ltrans"):
        copies[name].start()
    for c in place_copies:
        c.start()
    for name in ("dtrans", "lcoup", "dcoup", "gcoup"):
        copies[name].start()

    barrier = pltpu.get_barrier_semaphore()

    def hello(a, b):
        pl.semaphore_signal(barrier, inc=1, device_id=(a, b), device_id_type=MESH)

    for i, j in COLUMN:
        hello(lax.rem(lat + i, 4), lon + j * (1 - 2 * hi))
    for m in range(1, 16):
        hello(lat, at_lon(2 * m))
    hello(lat, at_lon(1))
    hello(lat, at_lon(-1))

    @pl.when(has_cross)
    def _():
        hello(cross, at_lon(1))
        hello(cross, at_lon(-1))

    pl.semaphore_wait(barrier, 7 + 15 + 2 + jnp.where(has_cross, 2, 0).astype(jnp.int32))

    def remote(name, src, dst, device):
        k = SEMS[name]
        return pltpu.make_async_remote_copy(
            src_ref=src, dst_ref=dst, send_sem=ssem.at[k], recv_sem=rsem.at[k], device_id=device, device_id_type=MESH
        )

    sends = {}

    def leaf_send(which, rho, col, dst_rho, dst_col, device):
        sends["loss", which] = remote(("loss", which), loss_h.at[leaf(rho, col)], ext.at[4 * dst_rho + dst_col], device)
        sends["place", which] = remote(("place", which), place_h.at[leaf(rho, col)], pext.at[4 * dst_rho + dst_col], device)

    for rho in (1, 2):
        leaf_send(f"lonp{rho}", rho, 2, rho, 0, (lat, at_lon(1)))
        leaf_send(f"lonm{rho}", rho, 1, rho, 3, (lat, at_lon(-1)))
    for b in (0, 1):
        leaf_send(f"part{b}", 2, 1 + b, 3, 1 + b, (partner, lon))
        leaf_send(f"cross{b}", 1, 1 + b, 0, 1 + b, (cross, lon))
    leaf_send("xcp", 1, 2, 0, 0, (cross, at_lon(1)))
    leaf_send("xcm", 1, 1, 0, 3, (cross, at_lon(-1)))
    for k, col in ((0, 0), (1, 3)):
        for kind, ref in (("loss", ext), ("place", pext)):
            sends[kind, f"fwd{k}"] = remote((kind, f"fwd{k}"), ref.at[4 * 2 + col], ref.at[4 * 3 + col], (partner, lon))
    own = coef.at[4]
    sends["coef", "lonp"] = remote(("coef", "lonp"), own, coef.at[3], (lat, at_lon(1)))
    sends["coef", "lonm"] = remote(("coef", "lonm"), own, coef.at[5], (lat, at_lon(-1)))
    sends["coef", "part"] = remote(("coef", "part"), own, coef.at[7], (partner, lon))
    sends["coef", "cross"] = remote(("coef", "cross"), own, coef.at[1], (cross, lon))
    sends["coef", "xcp"] = remote(("coef", "xcp"), own, coef.at[0], (cross, at_lon(1)))
    sends["coef", "xcm"] = remote(("coef", "xcm"), own, coef.at[2], (cross, at_lon(-1)))
    sends["coef", "fwd0"] = remote(("coef", "fwd0"), coef.at[3], coef.at[6], (partner, lon))
    sends["coef", "fwd1"] = remote(("coef", "fwd1"), coef.at[5], coef.at[8], (partner, lon))
    for i, j in COLUMN:
        mine = cellw.at[1, hi, lat]
        sends["cell", (i, j)] = remote(("cell", (i, j)), mine, mine, (lax.rem(lat + i, 4), lon + j * (1 - 2 * hi)))
    sends["win", "p"] = remote(("win", "p"), cellw.at[1], cellw.at[0], (lat, at_lon(2)))
    sends["win", "m"] = remote(("win", "m"), cellw.at[1], cellw.at[2], (lat, at_lon(-2)))
    for m in FAR:
        sends["group", m] = remote(("group", m), group, gall.at[m - 2], (lat, at_lon(2 * m)))

    def start(*names):
        for name in names:
            sends[name].start()

    def both(*whiches):
        return [(kind, which) for which in whiches for kind in ("place", "loss")]

    def recv(*names):
        for name in names:
            sends[name].wait_recv()

    start(*both("lonp2", "lonm2"))
    start(*both("part0", "part1"))

    @pl.when(has_cross)
    def _():
        start(*both("cross0", "cross1"))

    copies["basis"].wait()
    for k, (rho, col) in enumerate(own_slots):
        copies[f"ext{k}"].wait()
        l = leaf(rho, col)
        coef[4, l] = mm3(basis[l], ext[4 * rho + col], ((0,), (0,)))
    start(("coef", "lonp"), ("coef", "lonm"), ("coef", "part"))

    @pl.when(has_cross)
    def _():
        start(("coef", "cross"), ("coef", "xcp"), ("coef", "xcm"))

    copies["ltrans"].wait()
    cellw[1, hi, lat] = mm3(ltrans[...].reshape(256, 64), coef[4].reshape(256, 256), ((0,), (0,)))
    start(*[("cell", pair) for pair in COLUMN])
    start(*both("lonp1", "lonm1"))

    @pl.when(has_cross)
    def _():
        start(*both("xcp", "xcm"))

    @pl.when(jnp.logical_not(has_cross))
    def _():
        for k in range(3):
            coef[k] = jnp.zeros((4, 64, 256), f32)

    for c in place_copies:
        c.wait()

    def near_source(slot):
        def body(c, carry):
            rows = pl.ds(pl.multiple_of(c * 64, 64), 64)
            high, low = split(ext[slot, rows, :])
            sh[rows, :] = high
            sl[rows, :] = low
            return carry

        lax.fori_loop(0, 8, body, 0)

    def near_block(rho_s, col_s, rho_t, col_t):
        di = (rho_s - rho_t) * sign
        dj = col_s - col_t
        l = leaf(rho_t, col_t)
        slot = 4 * rho_s + col_s
        off = (1 - flags[l * 9 + 3 * (di + 1) + dj + 1]).astype(f32) * AWAY
        src_row = pext[slot, 0:1, :] + (di.astype(f32) * UNIT + off)
        src_col = pext[slot, 1:2, :] + dj.astype(f32) * UNIT

        def body(c, carry):
            rows = pl.ds(pl.multiple_of(c * 32, 32), 32)
            target = column_ref[l, rows, :]
            dr = target[:, 0:1] - src_row
            dc = target[:, 1:2] - src_col
            sq = dr * dr + dc * dc
            u = sq * lax.rsqrt(jnp.maximum(sq, 1e-30))
            k = (1.0 + u * LN2) * jnp.exp2(-u)
            high, low = split(k)
            kh[rows, :] = high
            kl[rows, :] = low
            return carry

        lax.fori_loop(0, 16, body, 0)

        def product(c, carry):
            rows = pl.ds(pl.multiple_of(c * 256, 256), 256)
            high = kh[rows, :]
            acc[l, rows, :] += mm(high, sh[...]) + mm(kl[rows, :], sh[...]) + mm(high, sl[...])
            return carry

        lax.fori_loop(0, 2, product, 0)

    as_i32 = lambda v: jnp.asarray(v, jnp.int32)

    for k, (rho, col) in enumerate(own_slots):
        acc[leaf(rho, col)] = 0.5 * ext[4 * rho + col]

    def own_body(i, carry):
        rho_s, col_s = 1 + i // 2, 1 + i % 2
        near_source(4 * rho_s + col_s)

        def inner(t, c):
            near_block(rho_s, col_s, 1 + t // 2, 1 + t % 2)
            return c

        return lax.fori_loop(0, 4, inner, carry)

    def pair_sources(rho_s, col_of, targets):
        def outer(i, carry):
            col_s = col_of(i)
            near_source(4 * rho_s + col_s)

            def inner(t, c):
                rho_t, col_t = targets(i, t)
                near_block(as_i32(rho_s), col_s, as_i32(rho_t), col_t)
                return c

            return lax.fori_loop(0, 2, inner, carry)

        lax.fori_loop(0, 2, outer, 0)

    def corner_sources(rho_s, rho_t):
        def outer(i, carry):
            near_source(4 * rho_s + 3 * i)
            near_block(as_i32(rho_s), 3 * i, as_i32(rho_t), 1 + i)
            return carry

        lax.fori_loop(0, 2, outer, 0)

    lax.fori_loop(0, 4, own_body, 0)

    copies["dtrans"].wait()
    recv(*[("cell", pair) for pair in COLUMN])
    start(("win", "p"), ("win", "m"))
    for g in range(2):
        total = jnp.zeros((64, 256), f32)
        for f in range(2):
            total += mm3(
                dtrans[2 * g : 2 * g + 2, f].reshape(128, 64), cellw[1, f, 2 * g : 2 * g + 2].reshape(128, 256), ((0,), (0,))
            )
        group[g] = total
    start(*[("group", m) for m in FAR])

    recv(("coef", "lonp"), ("coef", "lonm"))
    start(("coef", "fwd0"), ("coef", "fwd1"))
    recv(*both("lonp2", "lonm2"))
    start(*both("fwd0", "fwd1"))
    recv(*both("part0", "part1"))
    pair_sources(3, lambda i: 1 + i, lambda i, t: (2, 1 + t))
    pair_sources(2, lambda i: 3 * i, lambda i, t: (1 + t, 1 + i))

    @pl.when(has_cross)
    def _():
        recv(*both("cross0", "cross1"))
        pair_sources(0, lambda i: 1 + i, lambda i, t: (1, 1 + t))

    copies["dcoup"].wait()
    copies["gcoup"].wait()
    copies["lcoup"].wait()
    recv(("win", "p"), ("win", "m"))

    def window_body(i, total):
        v, row = i // 4, i % 4
        hoff, f = v // 2, v % 2
        w = 6 * (row + 2 - 2 * row_group) + v
        away = (jnp.abs(row - lat) > 1) | (jnp.abs(v - 2 - hi) > 1)
        keep = jnp.where(away, 1.0, 0.0)
        weight = (dcoup[w].astype(f32) * keep).astype(bf16)
        return total + mm2(weight, cellw[hoff, f, row])

    device_far = lax.fori_loop(0, 24, window_body, jnp.zeros((64, 256), f32))
    recv(*[("group", m) for m in FAR])

    def group_body(i, total):
        m, g = i // 2, i % 2
        other = lax.rem(col_group - (m + 2) + 16, 16)
        return total + mm2(gcoup[g, other], gall[m, g])

    group_field = lax.fori_loop(0, 26, group_body, jnp.zeros((64, 256), f32))
    device_field = device_far + mm3(dtrans[lat, hi], group_field)
    recv(("coef", "part"), ("coef", "fwd0"), ("coef", "fwd1"))

    @pl.when(has_cross)
    def _():
        recv(("coef", "cross"), ("coef", "xcp"), ("coef", "xcm"))

    field[...] = mm3(ltrans[...].reshape(256, 64), device_field)

    def leaf_body(w, carry):
        u, v = w // 6, w % 6
        side = u // 2
        slot = 3 * (side + par * (2 - 2 * side)) + v // 2
        weights = []
        for l in range(4):
            di, dj = u - 2 - l // 2, v - 2 - l % 2
            inside = (jnp.abs(di) <= 1) & (jnp.abs(dj) <= 1)
            index = l * 9 + 3 * (jnp.clip(di, -1, 1) + 1) + jnp.clip(dj, -1, 1) + 1
            keep = (1 - flags[index] * jnp.where(inside, 1, 0)).astype(f32)
            weights.append((lcoup[l, w].astype(f32) * keep).astype(bf16))
        field[...] += mm2(jnp.concatenate(weights, 0), coef[slot, 2 * (u % 2) + v % 2])
        return carry

    lax.fori_loop(0, 36, leaf_body, 0)

    recv(*both("lonp1", "lonm1"))
    pair_sources(1, lambda i: 3 * i, lambda i, t: (1 + t, 1 + i))
    recv(*both("fwd0", "fwd1"))
    corner_sources(3, 2)

    @pl.when(has_cross)
    def _():
        recv(*both("xcp", "xcm"))
        corner_sources(0, 1)

    outs = []
    for l in range(4):
        acc[l] += mm3(basis[l], field[pl.ds(64 * l, 64), :])
        c = pltpu.make_async_copy(acc.at[l], out_h.at[l], osem.at[l])
        c.start()
        outs.append(c)
    for c in outs:
        c.wait()
    crossing = [("coef", w) for w in ("cross", "xcp", "xcm")] + both("cross0", "cross1", "xcp", "xcm")
    for name in sends:
        if name not in crossing:
            sends[name].wait_send()

    @pl.when(has_cross)
    def _():
        for name in crossing:
            sends[name].wait_send()


def local(losses, positions, leaf_basis, near_flags, leaf_coupling, leaf_transfer, device_coupling, device_transfer, group_coupling):
    places = (positions * UNIT).reshape(4, 2, 512)
    rows = jnp.pad(places, ((0, 0), (0, 6), (0, 0)))
    columns = jnp.transpose(places, (0, 2, 1))
    anywhere = pl.BlockSpec(memory_space=pl.ANY)
    vmem = pltpu.VMEM
    out = pl.pallas_call(
        kernel,
        out_shape=jax.ShapeDtypeStruct((4, 512, 256), f32),
        in_specs=[anywhere, anywhere, pl.BlockSpec(memory_space=pltpu.VMEM), pl.BlockSpec(memory_space=pltpu.SMEM)] + [anywhere] * 6,
        out_specs=anywhere,
        scratch_shapes=[
            vmem((16, 512, 256), f32), vmem((16, 8, 512), f32), vmem((9, 4, 64, 256), f32),
            vmem((3, 2, 4, 64, 256), f32), vmem((2, 64, 256), f32), vmem((13, 2, 64, 256), f32),
            vmem((4, 512, 256), f32), vmem((512, 512), bf16), vmem((512, 512), bf16),
            vmem((512, 256), bf16), vmem((512, 256), bf16), vmem((256, 256), f32),
            vmem((4, 512, 64), f32), vmem((4, 36, 64, 64), bf16), vmem((4, 64, 64), f32),
            vmem((36, 64, 64), bf16), vmem((4, 2, 64, 64), f32), vmem((2, 16, 64, 64), bf16),
            pltpu.SemaphoreType.DMA((14,)), pltpu.SemaphoreType.DMA((4,)),
            pltpu.SemaphoreType.DMA((len(SEMS),)), pltpu.SemaphoreType.DMA((len(SEMS),)),
        ],
        compiler_params=pltpu.CompilerParams(collective_id=0, has_side_effects=True, vmem_limit_bytes=60 * 1024 * 1024),
        name="apply",
    )(
        losses.reshape(4, 512, 256), rows, columns, near_flags.reshape(36), leaf_basis.reshape(4, 512, 64),
        leaf_coupling.reshape(4, 36, 64, 64), leaf_transfer.reshape(4, 64, 64), device_coupling.reshape(36, 64, 64),
        device_transfer, group_coupling,
    )
    return out.reshape(2, 2, 512, 256)


def solution(mesh):
    placed = (
        P("lat", "lon", None, None),
        P("lat", "lon", None, None),
        P("lat", "lon", None, None),
        P("lat", "lon", None),
        P("lat", "lon", None, None, None),
        P("lat", "lon", None, None),
        P("lat", "lon", None, None, None),
        P(),
        P(),
    )
    return jax.shard_map(
        local, mesh=mesh, in_specs=placed, out_specs=P("lat", "lon", None, None), check_vma=False
    )
```

```python
import jax
import jax.numpy as jnp
from jax import lax
from jax.experimental import pallas as pl
from jax.experimental.pallas import tpu as pltpu
from jax.sharding import PartitionSpec as P

MESH = pl.DeviceIdType.MESH
LOG2E = 1.4426950408889634
UNIT = 1.7320508075688772 / 0.15
AWAY = 1.0e4
f32, bf16 = jnp.float32, jnp.bfloat16


def split(x):
    high = x.astype(bf16)
    return high, (x - high.astype(f32)).astype(bf16)


def mm(a, b, dims=((1,), (0,))):
    return lax.dot_general(a, b, (dims, ((), ())), preferred_element_type=f32)


def mm3(a, b, dims=((1,), (0,))):
    ah, al = split(a)
    bh, bl = split(b)
    return mm(ah, bh, dims) + mm(al, bh, dims) + mm(ah, bl, dims)


def mm2(a, b):
    bh, bl = split(b)
    return mm(a, bh) + mm(a, bl)


FAR = tuple(range(2, 15))
COLUMN = ((2, 0), (0, 1), (2, 1))


def remote_names():
    names = []
    for kind in ("loss", "place"):
        for which in ("lonp1", "lonp2", "lonm1", "lonm2", "part0", "part1", "cross0", "cross1", "xcp", "xcm", "fwd0", "fwd1"):
            names.append((kind, which))
    for which in ("lonp", "lonm", "part", "cross", "xcp", "xcm", "fwd0", "fwd1"):
        names.append(("coef", which))
    for pair in COLUMN:
        names += [("cell", pair), ("cellf", pair)]
    names += [("cell", "part"), ("win", 0), ("winf", 0), ("sum", 0)]
    for m in FAR:
        names.append(("group", m))
    return {name: k for k, name in enumerate(names)}


SEMS = remote_names()


def kernel(
    loss_h, place_h, flags, basis_h, lcoup_h, ltrans_h, dcoup_h, dtrans_h, gcoup_h,
    out_h,
    ext, pext, coef, cellw, group, gall, part, acc, ka_h, ka_l, kb_h, kb_l, sh, sl, field, columns,
    basis, lcoup, ltrans, dcoup, dtrans, gcoup,
    lsem, osem, ssem, rsem,
):
    lat, lon = lax.axis_index("lat"), lax.axis_index("lon")
    n_lon = lax.axis_size("lon")
    par, hi = lax.rem(lat, 2), lax.rem(lon, 2)
    row_group, col_group = lat // 2, lon // 2
    sign = 1 - 2 * par
    has_cross = (lat == 1) | (lat == 2)
    partner, cross = lat + sign, lat - sign

    def leaf(rho, col):
        return 2 * (par + (rho - 1) * sign) + (col - 1)

    def at_lon(step):
        return lax.rem(lon + step + n_lon, n_lon)

    def local(src, dst, k):
        return pltpu.make_async_copy(src, dst, lsem.at[k])

    own_slots = [(1, 1), (1, 2), (2, 1), (2, 2)]
    copies = {}
    for k, (rho, col) in enumerate(own_slots):
        copies[f"ext{k}"] = local(loss_h.at[leaf(rho, col)], ext.at[4 * rho + col], k)
    for k, (src, dst, name) in enumerate((
        (basis_h, basis, "basis"), (lcoup_h, lcoup, "lcoup"), (ltrans_h, ltrans, "ltrans"),
        (dcoup_h, dcoup, "dcoup"), (dtrans_h.at[:, pl.ds(2 * col_group, 2)], dtrans, "dtrans"),
        (gcoup_h.at[row_group, col_group, par], gcoup, "gcoup"),
    )):
        copies[name] = local(src, dst, 4 + k)
    place_copies = [
        local(place_h.at[leaf(rho, col)], pext.at[4 * rho + col], 10 + k) for k, (rho, col) in enumerate(own_slots)
    ]
    for k in range(4):
        copies[f"ext{k}"].start()
    for name in ("basis", "ltrans"):
        copies[name].start()
    for c in place_copies:
        c.start()
    for name in ("dtrans", "lcoup", "dcoup", "gcoup"):
        copies[name].start()

    barrier = pltpu.get_barrier_semaphore()

    def hello(a, b):
        pl.semaphore_signal(barrier, inc=1, device_id=(a, b), device_id_type=MESH)

    flip = 1 - 2 * hi
    for i, j in COLUMN:
        hello(lax.rem(lat + i, 4), lon + j * flip)
    hello(partner, lon)
    for m in range(1, 16):
        hello(lat, at_lon(2 * m))
    hello(lat, at_lon(1))
    hello(lat, at_lon(-1))

    @pl.when(has_cross)
    def _():
        hello(cross, lon)
        hello(cross, at_lon(1))
        hello(cross, at_lon(-1))

    pl.semaphore_wait(barrier, 4 + 15 + 2 + jnp.where(has_cross, 3, 0).astype(jnp.int32))

    def remote(name, src, dst, device):
        k = SEMS[name]
        return pltpu.make_async_remote_copy(
            src_ref=src, dst_ref=dst, send_sem=ssem.at[k], recv_sem=rsem.at[k], device_id=device, device_id_type=MESH
        )

    sends = {}

    def leaf_send(which, rho, col, dst_rho, dst_col, device):
        sends["loss", which] = remote(("loss", which), loss_h.at[leaf(rho, col)], ext.at[4 * dst_rho + dst_col], device)
        sends["place", which] = remote(("place", which), place_h.at[leaf(rho, col)], pext.at[4 * dst_rho + dst_col], device)

    for rho in (1, 2):
        leaf_send(f"lonp{rho}", rho, 2, rho, 0, (lat, at_lon(1)))
        leaf_send(f"lonm{rho}", rho, 1, rho, 3, (lat, at_lon(-1)))
    for b in (0, 1):
        leaf_send(f"part{b}", 2, 1 + b, 3, 1 + b, (partner, lon))
        leaf_send(f"cross{b}", 1, 1 + b, 0, 1 + b, (cross, lon))
    leaf_send("xcp", 1, 2, 0, 0, (cross, at_lon(1)))
    leaf_send("xcm", 1, 1, 0, 3, (cross, at_lon(-1)))
    for k, col in ((0, 0), (1, 3)):
        for kind, ref in (("loss", ext), ("place", pext)):
            sends[kind, f"fwd{k}"] = remote((kind, f"fwd{k}"), ref.at[4 * 2 + col], ref.at[4 * 3 + col], (partner, lon))
    own = coef.at[4]
    sends["coef", "lonp"] = remote(("coef", "lonp"), own, coef.at[3], (lat, at_lon(1)))
    sends["coef", "lonm"] = remote(("coef", "lonm"), own, coef.at[5], (lat, at_lon(-1)))
    sends["coef", "part"] = remote(("coef", "part"), own, coef.at[7], (partner, lon))
    sends["coef", "cross"] = remote(("coef", "cross"), own, coef.at[1], (cross, lon))
    sends["coef", "xcp"] = remote(("coef", "xcp"), own, coef.at[0], (cross, at_lon(1)))
    sends["coef", "xcm"] = remote(("coef", "xcm"), own, coef.at[2], (cross, at_lon(-1)))
    sends["coef", "fwd0"] = remote(("coef", "fwd0"), coef.at[3], coef.at[6], (partner, lon))
    sends["coef", "fwd1"] = remote(("coef", "fwd1"), coef.at[5], coef.at[8], (partner, lon))
    for i, j in COLUMN:
        mine = cellw.at[1, hi, lat]
        sends["cell", (i, j)] = remote(("cell", (i, j)), mine, mine, (lax.rem(lat + i, 4), lon + j * flip))
        theirs = cellw.at[1, lax.rem(hi + j, 2), lax.rem(lat + i, 4)]
        sends["cellf", (i, j)] = remote(("cellf", (i, j)), theirs, theirs, (partner, lon))
    sends["cell", "part"] = remote(("cell", "part"), cellw.at[1, hi, lat], cellw.at[1, hi, lat], (partner, lon))
    sends["win", 0] = remote(("win", 0), cellw.at[1], cellw.at[2 * par], (lat, at_lon(2 * sign)))
    sends["winf", 0] = remote(("winf", 0), cellw.at[2 * par], cellw.at[2 * par], (partner, lon))
    for m in FAR:
        sends["group", m] = remote(("group", m), group, gall.at[m - 2], (lat, at_lon(2 * m)))
    sends["sum", 0] = remote(("sum", 0), part.at[0], part.at[1], (partner, lon))

    def start(*names):
        for name in names:
            sends[name].start()

    def both(*whiches):
        return [(kind, which) for which in whiches for kind in ("place", "loss")]

    def only(kind, *whiches):
        return [(kind, which) for which in whiches]

    def recv(*names):
        for name in names:
            sends[name].wait_recv()

    start(*only("place", "lonp2", "lonm2", "part0", "part1", "lonp1", "lonm1"))
    start(*only("loss", "part0", "part1", "lonp2", "lonm2"))

    @pl.when(has_cross)
    def _():
        start(*only("place", "cross0", "cross1", "xcp", "xcm"))

    copies["basis"].wait()
    for k, (rho, col) in enumerate(own_slots):
        copies[f"ext{k}"].wait()
        l = leaf(rho, col)
        coef[4, l] = mm3(basis[l], ext[4 * rho + col], ((0,), (0,)))
    copies["ltrans"].wait()
    cellw[1, hi, lat] = mm3(ltrans[...].reshape(256, 64), coef[4].reshape(256, 256), ((0,), (0,)))
    start(("cell", "part"), *[("cell", pair) for pair in COLUMN])
    start(("coef", "lonp"), ("coef", "lonm"), ("coef", "part"))

    @pl.when(has_cross)
    def _():
        start(("coef", "cross"), ("coef", "xcp"), ("coef", "xcm"))
        start(*only("loss", "cross0", "cross1", "xcp", "xcm"))

    @pl.when(jnp.logical_not(has_cross))
    def _():
        for k in range(3):
            coef[k] = jnp.zeros((4, 64, 256), f32)

    for c in place_copies:
        c.wait()

    for rho, col in own_slots:
        for axis in range(2):
            row = pext[4 * rho + col, axis : axis + 1, :] * UNIT
            columns[leaf(rho, col), axis] = jnp.transpose(jnp.broadcast_to(row, (128, 512)))

    def near_source(slot):
        def body(c, carry):
            rows = pl.ds(pl.multiple_of(c * 64, 64), 64)
            high, low = split(ext[slot, rows, :])
            sh[slot, rows, :] = high
            sl[slot, rows, :] = low
            return carry

        lax.fori_loop(0, 8, body, 0)

    def near_kernel(pair, half, high_ref, low_ref):
        rho_s, col_s, rho_t, col_t = pair
        di = (rho_s - rho_t) * sign
        dj = col_s - col_t
        l = leaf(rho_t, col_t)
        slot = 4 * rho_s + col_s
        off = (1 - flags[l * 9 + 3 * (di + 1) + dj + 1]).astype(f32) * AWAY
        src_row = (pext[slot, 0:1, :] + di.astype(f32)) * UNIT + off
        src_col = (pext[slot, 1:2, :] + dj.astype(f32)) * UNIT
        for c in range(4):
            rows = slice(64 * c, 64 * c + 64)
            for j in range(4):
                lanes = slice(128 * j, 128 * j + 128)
                dr = columns[l, 0, 256 * half + 64 * c : 256 * half + 64 * c + 64, :] - src_row[:, lanes]
                dc = columns[l, 1, 256 * half + 64 * c : 256 * half + 64 * c + 64, :] - src_col[:, lanes]
                sq = dr * dr + dc * dc
                d = sq * lax.rsqrt(jnp.maximum(sq, 1e-30))
                k = (1.0 + d) * jnp.exp2(d * -LOG2E)
                high, low = split(k)
                high_ref[rows, lanes] = high
                low_ref[rows, lanes] = low

    def near_product(pair, half, high_ref, low_ref):
        rho_s, col_s, rho_t, col_t = pair
        l = leaf(rho_t, col_t)
        slot = 4 * rho_s + col_s
        high = high_ref[...]
        source = sh[slot]
        acc[l, 256 * half : 256 * half + 256, :] += mm(high, source) + mm(low_ref[...], source) + mm(high, sl[slot])

    def near(count, pair_of):
        def typed(i):
            return tuple(jnp.asarray(v, jnp.int32) for v in pair_of(i))

        near_kernel(typed(jnp.int32(0)), 0, ka_h, ka_l)

        def body(i, carry):
            pair = typed(i)
            near_kernel(pair, 1, kb_h, kb_l)
            near_product(pair, 0, ka_h, ka_l)
            near_kernel(typed(jnp.minimum(i + 1, count - 1)), 0, ka_h, ka_l)
            near_product(pair, 1, kb_h, kb_l)
            return carry

        lax.fori_loop(0, count, body, 0)

    def split_all(*slots):
        for slot in slots:
            near_source(slot)

    for k, (rho, col) in enumerate(own_slots):
        acc[leaf(rho, col)] = 0.5 * ext[4 * rho + col]
    split_all(5, 6, 9, 10)
    near(16, lambda i: (1 + i // 8, 1 + (i // 4) % 2, 1 + (i // 2) % 2, 1 + i % 2))
    recv(*[("cell", pair) for pair in COLUMN])
    start(*[("cellf", pair) for pair in COLUMN])
    recv(*both("part0", "part1"))
    split_all(13, 14)
    near(4, lambda i: (3, 1 + i // 2, 2, 1 + i % 2))

    copies["dtrans"].wait()
    recv(("cell", "part"), *[("cellf", pair) for pair in COLUMN])
    start(("win", 0))
    first = 2 * par
    total = jnp.zeros((64, 256), f32)
    for f in range(2):
        for e in range(2):
            total += mm3(dtrans[first + e, f], cellw[1, f, first + e], ((0,), (0,)))
    group[...] = total
    start(*[("group", m) for m in FAR])
    start(*only("loss", "lonp1", "lonm1"))

    recv(("coef", "lonp"), ("coef", "lonm"))
    start(("coef", "fwd0"), ("coef", "fwd1"))
    recv(*both("lonp2", "lonm2"))
    start(*both("fwd0", "fwd1"))
    split_all(8, 11)
    near(4, lambda i: (2, 3 * (i // 2), 1 + i % 2, 1 + i // 2))
    recv(("win", 0))
    start(("winf", 0))

    copies["dcoup"].wait()
    copies["gcoup"].wait()
    copies["lcoup"].wait()
    recv(*[("group", m) for m in FAR])
    total = jnp.zeros((64, 256), f32)
    for m in FAR:
        total += mm2(gcoup[lax.rem(col_group - m + 16, 16)], gall[m - 2])
    part[0] = total
    start(("sum", 0))

    @pl.when(has_cross)
    def _():
        recv(*both("cross0", "cross1"))
        split_all(1, 2)
        near(4, lambda i: (0, 1 + i // 2, 1, 1 + i % 2))

    recv(("winf", 0))

    def window_body(v, total):
        hoff, f = v // 2, v % 2
        for row in range(4):
            w = 6 * (row + 2 - 2 * row_group) + v
            away = (jnp.abs(row - lat) > 1) | (jnp.abs(v - 2 - hi) > 1)
            keep = jnp.where(away, 1.0, 0.0)
            weight = (dcoup[w].astype(f32) * keep).astype(bf16)
            total += mm2(weight, cellw[hoff, f, row])
        return total

    device_far = lax.fori_loop(0, 6, window_body, jnp.zeros((64, 256), f32))
    recv(("sum", 0))
    device_field = device_far + mm3(dtrans[lat, hi], part[0] + part[1])
    recv(("coef", "part"), ("coef", "fwd0"), ("coef", "fwd1"))

    @pl.when(has_cross)
    def _():
        recv(("coef", "cross"), ("coef", "xcp"), ("coef", "xcm"))

    field[...] = mm3(ltrans[...].reshape(256, 64), device_field)

    def leaf_body(i, carry):
        side, v_side = i // 3, i % 3
        slot = 3 * (side + par * (2 - 2 * side)) + v_side
        total = field[...]
        for a in range(2):
            for b in range(2):
                u, v = 2 * side + a, 2 * v_side + b
                w = 6 * u + v
                weights = []
                for l in range(4):
                    di, dj = u - 2 - l // 2, v - 2 - l % 2
                    inside = (jnp.abs(di) <= 1) & (jnp.abs(dj) <= 1)
                    index = l * 9 + 3 * (jnp.clip(di, -1, 1) + 1) + jnp.clip(dj, -1, 1) + 1
                    keep = (1 - flags[index] * jnp.where(inside, 1, 0)).astype(f32)
                    weights.append((lcoup[l, w].astype(f32) * keep).astype(bf16))
                total += mm2(jnp.concatenate(weights, 0), coef[slot, 2 * a + b])
        field[...] = total
        return carry

    lax.fori_loop(0, 9, leaf_body, 0)
    for l in range(4):
        acc[l] += mm3(basis[l], field[pl.ds(64 * l, 64), :])

    @pl.when(has_cross)
    def _():
        recv(*both("xcp", "xcm"))
        split_all(0, 3)
        near(2, lambda i: (0, 3 * i, 1, 1 + i))

    recv(*both("fwd0", "fwd1"))
    split_all(12, 15)
    near(2, lambda i: (3, 3 * i, 2, 1 + i))
    recv(*both("lonp1", "lonm1"))
    split_all(4, 7)
    near(4, lambda i: (1, 3 * (i // 2), 1 + i % 2, 1 + i // 2))

    outs = []
    for l in range(4):
        c = pltpu.make_async_copy(acc.at[l], out_h.at[l], osem.at[l])
        c.start()
        outs.append(c)
    for c in outs:
        c.wait()
    crossing = [("coef", w) for w in ("cross", "xcp", "xcm")] + both("cross0", "cross1", "xcp", "xcm")
    for name in sends:
        if name not in crossing:
            sends[name].wait_send()

    @pl.when(has_cross)
    def _():
        for name in crossing:
            sends[name].wait_send()


def local(losses, positions, leaf_basis, near_flags, leaf_coupling, leaf_transfer, device_coupling, device_transfer, group_coupling):
    anywhere = pl.BlockSpec(memory_space=pl.ANY)
    vmem = pltpu.VMEM
    out = pl.pallas_call(
        kernel,
        out_shape=jax.ShapeDtypeStruct((4, 512, 256), f32),
        in_specs=[anywhere, anywhere, pl.BlockSpec(memory_space=pltpu.SMEM)] + [anywhere] * 6,
        out_specs=anywhere,
        scratch_shapes=[
            vmem((16, 512, 256), f32), vmem((16, 2, 512), f32), vmem((9, 4, 64, 256), f32),
            vmem((3, 2, 4, 64, 256), f32), vmem((64, 256), f32), vmem((13, 64, 256), f32), vmem((2, 64, 256), f32),
            vmem((4, 512, 256), f32), vmem((256, 512), bf16), vmem((256, 512), bf16),
            vmem((256, 512), bf16), vmem((256, 512), bf16),
            vmem((16, 512, 256), bf16), vmem((16, 512, 256), bf16), vmem((256, 256), f32), vmem((4, 2, 512, 128), f32),
            vmem((4, 512, 64), f32), vmem((4, 36, 64, 64), bf16), vmem((4, 64, 64), f32),
            vmem((36, 64, 64), bf16), vmem((4, 2, 64, 64), f32), vmem((16, 64, 64), bf16),
            pltpu.SemaphoreType.DMA((14,)), pltpu.SemaphoreType.DMA((4,)),
            pltpu.SemaphoreType.DMA((len(SEMS),)), pltpu.SemaphoreType.DMA((len(SEMS),)),
        ],
        compiler_params=pltpu.CompilerParams(collective_id=0, has_side_effects=True, vmem_limit_bytes=60 * 1024 * 1024),
        name="apply",
    )(
        losses.reshape(4, 512, 256), positions.reshape(4, 2, 512), near_flags.reshape(36), leaf_basis.reshape(4, 512, 64),
        leaf_coupling.reshape(4, 36, 64, 64), leaf_transfer.reshape(4, 64, 64), device_coupling.reshape(36, 64, 64),
        device_transfer, group_coupling,
    )
    return out.reshape(2, 2, 512, 256)


def solution(mesh):
    placed = (
        P("lat", "lon", None, None),
        P("lat", "lon", None, None),
        P("lat", "lon", None, None),
        P("lat", "lon", None),
        P("lat", "lon", None, None, None),
        P("lat", "lon", None, None),
        P("lat", "lon", None, None, None),
        P(),
        P(),
    )
    return jax.shard_map(
        local, mesh=mesh, in_specs=placed, out_specs=P("lat", "lon", None, None), check_vma=False
    )
```

```python
import jax
import jax.numpy as jnp
from jax import lax
from jax.experimental import pallas as pl
from jax.experimental.pallas import tpu as pltpu
from jax.sharding import PartitionSpec as P

MESH = pl.DeviceIdType.MESH
LOG2E = 1.4426950408889634
UNIT = 1.7320508075688772 / 0.15
AWAY = 1.0e4
f32, bf16 = jnp.float32, jnp.bfloat16


def split(x):
    high = x.astype(bf16)
    return high, (x - high.astype(f32)).astype(bf16)


def mm(a, b, dims=((1,), (0,))):
    return lax.dot_general(a, b, (dims, ((), ())), preferred_element_type=f32)


def mm3(a, b, dims=((1,), (0,))):
    ah, al = split(a)
    bh, bl = split(b)
    return mm(ah, bh, dims) + mm(al, bh, dims) + mm(ah, bl, dims)


def mm2(a, b):
    bh, bl = split(b)
    return mm(a, bh) + mm(a, bl)


FAR = tuple(range(2, 15))
COLUMN = ((2, 0), (0, 1), (2, 1))


def remote_names():
    names = []
    for kind in ("loss", "place"):
        for which in ("lonp1", "lonp2", "lonm1", "lonm2", "part0", "part1", "cross0", "cross1", "xcp", "xcm", "fwd0", "fwd1", "relp", "relm"):
            names.append((kind, which))
    for which in ("lonp", "lonm", "part", "cross", "xcp", "xcm", "fwd0", "fwd1", "relp", "relm"):
        names.append(("coef", which))
    for pair in COLUMN:
        names += [("cell", pair), ("cellf", pair)]
    names += [("cell", "part"), ("win", 0), ("winf", 0), ("sum", 0)]
    for m in FAR:
        names.append(("group", m))
    return {name: k for k, name in enumerate(names)}


SEMS = remote_names()


def kernel(
    loss_h, place_h, flags, basis_h, lcoup_h, ltrans_h, dcoup_h, dtrans_h, gcoup_h,
    acc,
    ext, pext, coef, cellw, group, gall, part, ka_h, ka_l, kb_h, kb_l, sh, sl, field, columns,
    basis, lcoup, ltrans, dcoup, dtrans, gcoup,
    lsem, ssem, rsem,
):
    lat, lon = lax.axis_index("lat"), lax.axis_index("lon")
    n_lon = lax.axis_size("lon")
    par, hi = lax.rem(lat, 2), lax.rem(lon, 2)
    row_group, col_group = lat // 2, lon // 2
    sign = 1 - 2 * par
    has_cross = (lat == 1) | (lat == 2)
    partner, cross = lat + sign, lat - sign

    def leaf(rho, col):
        return 2 * (par + (rho - 1) * sign) + (col - 1)

    def at_lon(step):
        return lax.rem(lon + step + n_lon, n_lon)

    def local(src, dst, k):
        return pltpu.make_async_copy(src, dst, lsem.at[k])

    own_slots = [(1, 1), (1, 2), (2, 1), (2, 2)]
    copies = {}
    for k, (rho, col) in enumerate(own_slots):
        copies[f"ext{k}"] = local(loss_h.at[leaf(rho, col)], ext.at[4 * rho + col], k)
    for k, (src, dst, name) in enumerate((
        (basis_h, basis, "basis"), (lcoup_h, lcoup, "lcoup"), (ltrans_h, ltrans, "ltrans"),
        (dcoup_h, dcoup, "dcoup"), (dtrans_h.at[:, pl.ds(2 * col_group, 2)], dtrans, "dtrans"),
        (gcoup_h.at[row_group, col_group, par], gcoup, "gcoup"),
    )):
        copies[name] = local(src, dst, 4 + k)
    place_copies = [
        local(place_h.at[leaf(rho, col)], pext.at[4 * rho + col], 10 + k) for k, (rho, col) in enumerate(own_slots)
    ]
    for k in range(4):
        copies[f"ext{k}"].start()
    for name in ("basis", "ltrans"):
        copies[name].start()
    for c in place_copies:
        c.start()
    for name in ("dtrans", "lcoup", "dcoup", "gcoup"):
        copies[name].start()

    barrier = pltpu.get_barrier_semaphore()

    def hello(a, b):
        pl.semaphore_signal(barrier, inc=1, device_id=(a, b), device_id_type=MESH)

    flip = 1 - 2 * hi
    for i, j in COLUMN:
        hello(lax.rem(lat + i, 4), lon + j * flip)
    hello(partner, lon)
    for m in range(1, 16):
        hello(lat, at_lon(2 * m))
    hello(lat, at_lon(1))
    hello(lat, at_lon(-1))

    @pl.when(has_cross)
    def _():
        hello(cross, lon)
        hello(cross, at_lon(1))
        hello(cross, at_lon(-1))

    pl.semaphore_wait(barrier, 4 + 15 + 2 + jnp.where(has_cross, 3, 0).astype(jnp.int32))

    def remote(name, src, dst, device):
        k = SEMS[name]
        return pltpu.make_async_remote_copy(
            src_ref=src, dst_ref=dst, send_sem=ssem.at[k], recv_sem=rsem.at[k], device_id=device, device_id_type=MESH
        )

    sends = {}

    def leaf_send(which, rho, col, dst_rho, dst_col, device):
        sends["loss", which] = remote(("loss", which), loss_h.at[leaf(rho, col)], ext.at[4 * dst_rho + dst_col], device)
        sends["place", which] = remote(("place", which), place_h.at[leaf(rho, col)], pext.at[4 * dst_rho + dst_col], device)

    for rho in (1, 2):
        leaf_send(f"lonp{rho}", rho, 2, rho, 0, (lat, at_lon(1)))
        leaf_send(f"lonm{rho}", rho, 1, rho, 3, (lat, at_lon(-1)))
    for b in (0, 1):
        leaf_send(f"part{b}", 2, 1 + b, 3, 1 + b, (partner, lon))
        leaf_send(f"cross{b}", 1, 1 + b, 0, 1 + b, (cross, lon))
    leaf_send("xcp", 1, 2, 0, 0, (cross, at_lon(1)))
    leaf_send("xcm", 1, 1, 0, 3, (cross, at_lon(-1)))
    for k, col in ((0, 0), (1, 3)):
        for kind, ref in (("loss", ext), ("place", pext)):
            sends[kind, f"fwd{k}"] = remote((kind, f"fwd{k}"), ref.at[4 * 2 + col], ref.at[4 * 3 + col], (partner, lon))
    sends["loss", "relp"] = remote(("loss", "relp"), ext.at[0], ext.at[4], (cross, lon))
    sends["loss", "relm"] = remote(("loss", "relm"), ext.at[1], ext.at[7], (cross, at_lon(-1)))
    sends["coef", "relp"] = remote(("coef", "relp"), coef.at[0], coef.at[3], (cross, lon))
    sends["coef", "relm"] = remote(("coef", "relm"), coef.at[1], coef.at[5], (cross, at_lon(-1)))
    own = coef.at[4]
    sends["coef", "lonp"] = remote(("coef", "lonp"), own, coef.at[3], (lat, at_lon(1)))
    sends["coef", "lonm"] = remote(("coef", "lonm"), own, coef.at[5], (lat, at_lon(-1)))
    sends["coef", "part"] = remote(("coef", "part"), own, coef.at[7], (partner, lon))
    sends["coef", "cross"] = remote(("coef", "cross"), own, coef.at[1], (cross, lon))
    sends["coef", "xcp"] = remote(("coef", "xcp"), own, coef.at[0], (cross, at_lon(1)))
    sends["coef", "xcm"] = remote(("coef", "xcm"), own, coef.at[2], (cross, at_lon(-1)))
    sends["coef", "fwd0"] = remote(("coef", "fwd0"), coef.at[3], coef.at[6], (partner, lon))
    sends["coef", "fwd1"] = remote(("coef", "fwd1"), coef.at[5], coef.at[8], (partner, lon))
    for i, j in COLUMN:
        mine = cellw.at[1, hi, lat]
        sends["cell", (i, j)] = remote(("cell", (i, j)), mine, mine, (lax.rem(lat + i, 4), lon + j * flip))
        theirs = cellw.at[1, lax.rem(hi + j, 2), lax.rem(lat + i, 4)]
        sends["cellf", (i, j)] = remote(("cellf", (i, j)), theirs, theirs, (partner, lon))
    sends["cell", "part"] = remote(("cell", "part"), cellw.at[1, hi, lat], cellw.at[1, hi, lat], (partner, lon))
    sends["win", 0] = remote(("win", 0), cellw.at[1], cellw.at[2 * par], (lat, at_lon(2 * sign)))
    sends["winf", 0] = remote(("winf", 0), cellw.at[2 * par], cellw.at[2 * par], (partner, lon))
    for m in FAR:
        sends["group", m] = remote(("group", m), group, gall.at[m - 2], (lat, at_lon(2 * m)))
    sends["sum", 0] = remote(("sum", 0), part.at[0], part.at[1], (partner, lon))

    def start(*names):
        for name in names:
            sends[name].start()

    def both(*whiches):
        return [(kind, which) for which in whiches for kind in ("place", "loss")]

    def only(kind, *whiches):
        return [(kind, which) for which in whiches]

    def recv(*names):
        for name in names:
            sends[name].wait_recv()

    start(*only("place", "lonp2", "lonm2", "part0", "part1", "lonp1", "lonm1"))
    start(*only("loss", "part0", "part1", "lonp2", "lonm2"))

    @pl.when(has_cross)
    def _():
        start(*only("place", "cross0", "cross1", "xcp", "xcm"))

    copies["basis"].wait()
    for k, (rho, col) in enumerate(own_slots):
        copies[f"ext{k}"].wait()
        l = leaf(rho, col)
        coef[4, l] = mm3(basis[l], ext[4 * rho + col])
    copies["ltrans"].wait()
    cellw[1, hi, lat] = mm3(ltrans[...].reshape(256, 64), coef[4].reshape(256, 256), ((0,), (0,)))
    start(("cell", "part"), *[("cell", pair) for pair in COLUMN])
    start(("coef", "part"))

    @pl.when(has_cross)
    def _():
        start(("coef", "xcp"), ("coef", "cross"), ("coef", "xcm"))
        start(*only("loss", "xcp", "cross0", "cross1", "xcm"))

    @pl.when(jnp.logical_not(has_cross))
    def _():
        start(("coef", "lonp"), ("coef", "lonm"))
        for k in range(3):
            coef[k] = jnp.zeros((4, 64, 256), f32)

    for c in place_copies:
        c.wait()

    for rho, col in own_slots:
        for axis in range(2):
            row = pext[4 * rho + col, axis : axis + 1, :] * UNIT
            columns[leaf(rho, col), axis] = jnp.transpose(jnp.broadcast_to(row, (128, 512)))

    def near_source(slot):
        def body(c, carry):
            rows = pl.ds(pl.multiple_of(c * 64, 64), 64)
            high, low = split(ext[slot, rows, :])
            sh[slot, rows, :] = high
            sl[slot, rows, :] = low
            return carry

        lax.fori_loop(0, 8, body, 0)

    def near_kernel(pair, half, high_ref, low_ref):
        rho_s, col_s, rho_t, col_t = pair
        di = (rho_s - rho_t) * sign
        dj = col_s - col_t
        l = leaf(rho_t, col_t)
        slot = 4 * rho_s + col_s
        off = (1 - flags[l // 2, l % 2, 3 * (di + 1) + dj + 1]).astype(f32) * AWAY
        src_row = (pext[slot, 0:1, :] + di.astype(f32)) * UNIT + off
        src_col = (pext[slot, 1:2, :] + dj.astype(f32)) * UNIT
        for c in range(4):
            rows = slice(64 * c, 64 * c + 64)
            for j in range(4):
                lanes = slice(128 * j, 128 * j + 128)
                dr = columns[l, 0, 256 * half + 64 * c : 256 * half + 64 * c + 64, :] - src_row[:, lanes]
                dc = columns[l, 1, 256 * half + 64 * c : 256 * half + 64 * c + 64, :] - src_col[:, lanes]
                sq = dr * dr + dc * dc
                d = sq * lax.rsqrt(jnp.maximum(sq, 1e-30))
                k = (1.0 + d) * jnp.exp2(d * -LOG2E)
                high, low = split(k)
                high_ref[rows, lanes] = high
                low_ref[rows, lanes] = low

    def near_product(pair, half, high_ref, low_ref):
        rho_s, col_s, rho_t, col_t = pair
        l = leaf(rho_t, col_t)
        slot = 4 * rho_s + col_s
        high = high_ref[...]
        source = sh[slot]
        acc[l, 256 * half : 256 * half + 256, :] += mm(high, source) + mm(low_ref[...], source) + mm(high, sl[slot])

    def near(count, pair_of):
        def typed(i):
            return tuple(jnp.asarray(v, jnp.int32) for v in pair_of(i))

        near_kernel(typed(jnp.int32(0)), 0, ka_h, ka_l)

        def body(i, carry):
            pair = typed(i)
            near_kernel(pair, 1, kb_h, kb_l)
            near_product(pair, 0, ka_h, ka_l)
            near_kernel(typed(jnp.minimum(i + 1, count - 1)), 0, ka_h, ka_l)
            near_product(pair, 1, kb_h, kb_l)
            return carry

        lax.fori_loop(0, count, body, 0)

    def split_all(*slots):
        for slot in slots:
            near_source(slot)

    for k, (rho, col) in enumerate(own_slots):
        acc[leaf(rho, col)] = 0.5 * ext[4 * rho + col]
    split_all(5, 6, 9, 10)
    near(16, lambda i: (1 + i // 8, 1 + (i // 4) % 2, 1 + (i // 2) % 2, 1 + i % 2))
    recv(*[("cell", pair) for pair in COLUMN])
    start(*[("cellf", pair) for pair in COLUMN])
    recv(*both("part0", "part1"))
    split_all(13, 14)
    near(4, lambda i: (3, 1 + i // 2, 2, 1 + i % 2))

    copies["dtrans"].wait()
    recv(("cell", "part"), *[("cellf", pair) for pair in COLUMN])
    start(("win", 0))
    first = 2 * par
    total = jnp.zeros((64, 256), f32)
    for f in range(2):
        for e in range(2):
            total += mm3(dtrans[first + e, f], cellw[1, f, first + e], ((0,), (0,)))
    group[...] = total
    start(*[("group", m) for m in FAR])
    @pl.when(jnp.logical_not(has_cross))
    def _():
        start(*only("loss", "lonp1", "lonm1"))

    @pl.when(has_cross)
    def _():
        recv(("coef", "xcp"), ("coef", "cross"))
        start(("coef", "relp"), ("coef", "relm"))

    recv(*both("lonp2", "lonm2"))
    start(*both("fwd0", "fwd1"))
    split_all(8, 11)
    near(4, lambda i: (2, 3 * (i // 2), 1 + i % 2, 1 + i // 2))

    @pl.when(has_cross)
    def _():
        recv(*both("xcp", "cross0"))
        start(("loss", "relp"), ("loss", "relm"))
        recv(*both("cross1", "xcm"), ("coef", "relp"), ("coef", "relm"))

    @pl.when(jnp.logical_not(has_cross))
    def _():
        recv(("coef", "lonp"), ("coef", "lonm"))

    start(("coef", "fwd0"), ("coef", "fwd1"))
    recv(("win", 0))
    start(("winf", 0))

    @pl.when(has_cross)
    def _():
        split_all(0, 1, 2, 3)
        near(6, lambda i: (0, (i + 1) // 2, 1, jnp.where(i % 2 == 1, jnp.maximum(1, (i - 1) // 2), jnp.minimum(2, i // 2 + 1))))

    recv(*both("fwd0", "fwd1"))
    split_all(12, 15)
    near(2, lambda i: (3, 3 * i, 2, 1 + i))

    copies["dcoup"].wait()
    copies["gcoup"].wait()
    copies["lcoup"].wait()
    recv(("coef", "part"), ("coef", "fwd0"), ("coef", "fwd1"))

    @pl.when(has_cross)
    def _():
        recv(("coef", "xcm"))

    field[...] = jnp.zeros((256, 256), f32)

    def leaf_body(i, carry):
        side, v_side = i // 3, i % 3
        slot = 3 * (side + par * (2 - 2 * side)) + v_side
        total = field[...]
        for a in range(2):
            for b in range(2):
                u, v = 2 * side + a, 2 * v_side + b
                w = 6 * u + v
                weights = []
                for l in range(4):
                    di, dj = u - 2 - l // 2, v - 2 - l % 2
                    inside = (jnp.abs(di) <= 1) & (jnp.abs(dj) <= 1)
                    index = 3 * (jnp.clip(di, -1, 1) + 1) + jnp.clip(dj, -1, 1) + 1
                    keep = (1 - flags[l // 2, l % 2, index] * jnp.where(inside, 1, 0)).astype(f32)
                    weights.append((lcoup[l, w].astype(f32) * keep).astype(bf16))
                total += mm2(jnp.concatenate(weights, 0), coef[slot, 2 * a + b])
        field[...] = total
        return carry

    lax.fori_loop(0, 9, leaf_body, 0)
    recv(("winf", 0))

    def window_body(v, total):
        hoff, f = v // 2, v % 2
        for row in range(4):
            w = 6 * (row + 2 - 2 * row_group) + v
            away = (jnp.abs(row - lat) > 1) | (jnp.abs(v - 2 - hi) > 1)
            keep = jnp.where(away, 1.0, 0.0)
            weight = (dcoup[w].astype(f32) * keep).astype(bf16)
            total += mm2(weight, cellw[hoff, f, row])
        return total

    device_far = lax.fori_loop(0, 6, window_body, jnp.zeros((64, 256), f32))
    recv(*[("group", m) for m in FAR])
    total = jnp.zeros((64, 256), f32)
    for m in FAR:
        total += mm2(gcoup[lax.rem(col_group - m + 16, 16)], gall[m - 2])
    part[0] = total
    start(("sum", 0))
    recv(("sum", 0))
    device_field = device_far + mm3(dtrans[lat, hi], part[0] + part[1])
    field[...] += mm3(ltrans[...].reshape(256, 64), device_field)
    for l in range(4):
        acc[l] += mm3(basis[l], field[pl.ds(64 * l, 64), :], ((0,), (0,)))

    @pl.when(jnp.logical_not(has_cross))
    def _():
        recv(*only("loss", "lonp1", "lonm1"))

    @pl.when(has_cross)
    def _():
        recv(*only("loss", "relp", "relm"))

    recv(*only("place", "lonp1", "lonm1"))
    split_all(4, 7)
    near(4, lambda i: (1, 3 * (i // 2), 1 + i % 2, 1 + i // 2))

    crossing = [("coef", w) for w in ("cross", "xcp", "xcm", "relp", "relm")] + both("cross0", "cross1", "xcp", "xcm")
    crossing += only("loss", "relp", "relm")
    direct = [("coef", "lonp"), ("coef", "lonm")] + only("loss", "lonp1", "lonm1")
    for name in sends:
        if name not in crossing and name not in direct:
            sends[name].wait_send()

    @pl.when(has_cross)
    def _():
        for name in crossing:
            sends[name].wait_send()

    @pl.when(jnp.logical_not(has_cross))
    def _():
        for name in direct:
            sends[name].wait_send()


def local(losses, positions, leaf_basis, near_flags, leaf_coupling, leaf_transfer, device_coupling, device_transfer, group_coupling):
    anywhere = pl.BlockSpec(memory_space=pl.ANY)
    vmem = pltpu.VMEM
    call = pl.pallas_call(
        kernel,
        out_shape=jax.ShapeDtypeStruct((4, 512, 256), f32),
        in_specs=[anywhere, anywhere, pl.BlockSpec(memory_space=pltpu.SMEM)] + [anywhere] * 6,
        out_specs=pl.BlockSpec(memory_space=pltpu.VMEM),
        scratch_shapes=[
            vmem((16, 512, 256), f32), vmem((16, 2, 512), f32), vmem((9, 4, 64, 256), f32),
            vmem((3, 2, 4, 64, 256), f32), vmem((64, 256), f32), vmem((13, 64, 256), f32), vmem((2, 64, 256), f32),
            vmem((256, 512), bf16), vmem((256, 512), bf16),
            vmem((256, 512), bf16), vmem((256, 512), bf16),
            vmem((16, 512, 256), bf16), vmem((16, 512, 256), bf16), vmem((256, 256), f32), vmem((4, 2, 512, 128), f32),
            vmem((4, 64, 512), f32), vmem((4, 36, 64, 64), bf16), vmem((4, 64, 64), f32),
            vmem((36, 64, 64), bf16), vmem((4, 2, 64, 64), f32), vmem((16, 64, 64), bf16),
            pltpu.SemaphoreType.DMA((14,)),
            pltpu.SemaphoreType.DMA((len(SEMS),)), pltpu.SemaphoreType.DMA((len(SEMS),)),
        ],
        compiler_params=pltpu.CompilerParams(collective_id=0, has_side_effects=True, vmem_limit_bytes=40 * 1024 * 1024),
        name="apply",
    )
    hbm = lambda x: pltpu.with_memory_space_constraint(x, pltpu.HBM)
    out = call(
        hbm(losses.reshape(4, 512, 256)), hbm(positions.reshape(4, 2, 512)), near_flags,
        hbm(jnp.swapaxes(leaf_basis, 2, 3).reshape(4, 64, 512)), hbm(leaf_coupling.reshape(4, 36, 64, 64)),
        hbm(leaf_transfer.reshape(4, 64, 64)), hbm(device_coupling.reshape(36, 64, 64)), hbm(device_transfer), hbm(group_coupling),
    )
    return out.reshape(2, 2, 512, 256)


def solution(mesh):
    placed = (
        P("lat", "lon", None, None),
        P("lat", "lon", None, None),
        P("lat", "lon", None, None),
        P("lat", "lon", None),
        P("lat", "lon", None, None, None),
        P("lat", "lon", None, None),
        P("lat", "lon", None, None, None),
        P(),
        P(),
    )
    return jax.shard_map(
        local, mesh=mesh, in_specs=placed, out_specs=P("lat", "lon", None, None), check_vma=False
    )
```

```python
import jax
import jax.numpy as jnp
from jax import lax
from jax.experimental import pallas as pl
from jax.experimental.pallas import tpu as pltpu
from jax.sharding import PartitionSpec as P

MESH = pl.DeviceIdType.MESH
LOG2E = 1.4426950408889634
UNIT = 1.7320508075688772 / 0.15
AWAY = 1.0e4
f32, bf16 = jnp.float32, jnp.bfloat16


LOSS, PLACE, COEF, CELL, CELLF, WIN, WINF, GROUP, SUM = range(9)
LONP, LONM, LONP1, LONP2, LONM1, LONM2, PART, PART0, PART1, CROSS, CROSS0, CROSS1, XCP, XCM, FWD0, FWD1, RELP, RELM = range(18)
BASIS, LCOUP, LTRANS, DCOUP, DTRANS, GCOUP = range(10, 16)


def split(x):
    high = x.astype(bf16)
    return high, (x - high.astype(f32)).astype(bf16)


def mm(a, b, dims=((1,), (0,))):
    return lax.dot_general(a, b, (dims, ((), ())), preferred_element_type=f32)


def mm3(a, b, dims=((1,), (0,))):
    ah, al = split(a)
    bh, bl = split(b)
    return mm(ah, bh, dims) + mm(al, bh, dims) + mm(ah, bl, dims)


def mm2(a, b):
    bh, bl = split(b)
    return mm(a, bh) + mm(a, bl)


FAR = tuple(range(2, 15))
COLUMN = ((2, 0), (0, 1), (2, 1))


def remote_names():
    names = []
    for kind in (LOSS, PLACE):
        for which in (LONP1, LONP2, LONM1, LONM2, PART0, PART1, CROSS0, CROSS1, XCP, XCM, FWD0, FWD1, RELP, RELM):
            names.append((kind, which))
    for which in (LONP, LONM, PART, CROSS, XCP, XCM, FWD0, FWD1, RELP, RELM):
        names.append((COEF, which))
    for pair in COLUMN:
        names += [(CELL, pair), (CELLF, pair)]
    names += [(CELL, PART), (WIN, 0), (WINF, 0), (SUM, 0)]
    for m in FAR:
        names.append((GROUP, m))
    return {name: k for k, name in enumerate(names)}


SEMS = remote_names()


def kernel(
    loss_h, place_h, flags, basis_h, lcoup_h, ltrans_h, dcoup_h, dtrans_h, gcoup_h,
    acc,
    ext, pext, coef, cellw, group, gall, part, ka_h, ka_l, kb_h, kb_l, sh, sl, field, columns,
    basis, lcoup, ltrans, dcoup, dtrans, gcoup,
    lsem, ssem, rsem,
):
    lat, lon = lax.axis_index("lat"), lax.axis_index("lon")
    n_lon = lax.axis_size("lon")
    par, hi = lax.rem(lat, 2), lax.rem(lon, 2)
    row_group, col_group = lat // 2, lon // 2
    sign = 1 - 2 * par
    has_cross = (lat == 1) | (lat == 2)
    partner, cross = lat + sign, lat - sign

    def leaf(rho, col):
        return 2 * (par + (rho - 1) * sign) + (col - 1)

    def at_lon(step):
        return lax.rem(lon + step + n_lon, n_lon)

    def local(src, dst, k):
        return pltpu.make_async_copy(src, dst, lsem.at[k])

    own_slots = [(1, 1), (1, 2), (2, 1), (2, 2)]
    copies = {}
    for k, (rho, col) in enumerate(own_slots):
        copies[k] = local(loss_h.at[leaf(rho, col)], ext.at[4 * rho + col], k)
    for k, (src, dst, name) in enumerate((
        (basis_h, basis, BASIS), (lcoup_h, lcoup, LCOUP), (ltrans_h, ltrans, LTRANS),
        (dcoup_h, dcoup, DCOUP), (dtrans_h.at[:, pl.ds(2 * col_group, 2)], dtrans, DTRANS),
        (gcoup_h.at[row_group, col_group, par], gcoup, GCOUP),
    )):
        copies[name] = local(src, dst, 4 + k)
    place_copies = [
        local(place_h.at[leaf(rho, col)], pext.at[4 * rho + col], 10 + k) for k, (rho, col) in enumerate(own_slots)
    ]
    for k in range(4):
        copies[k].start()
    for name in (BASIS, LTRANS):
        copies[name].start()
    for c in place_copies:
        c.start()
    for name in (DTRANS, LCOUP, DCOUP, GCOUP):
        copies[name].start()

    barrier = pltpu.get_barrier_semaphore()

    def hello(a, b):
        pl.semaphore_signal(barrier, inc=1, device_id=(a, b), device_id_type=MESH)

    flip = 1 - 2 * hi
    for i, j in COLUMN:
        hello(lax.rem(lat + i, 4), lon + j * flip)
    hello(partner, lon)
    for m in range(1, 16):
        hello(lat, at_lon(2 * m))
    hello(lat, at_lon(1))
    hello(lat, at_lon(-1))

    @pl.when(has_cross)
    def _():
        hello(cross, lon)
        hello(cross, at_lon(1))
        hello(cross, at_lon(-1))

    pl.semaphore_wait(barrier, 4 + 15 + 2 + jnp.where(has_cross, 3, 0).astype(jnp.int32))

    def remote(name, src, dst, device):
        k = SEMS[name]
        return pltpu.make_async_remote_copy(
            src_ref=src, dst_ref=dst, send_sem=ssem.at[k], recv_sem=rsem.at[k], device_id=device, device_id_type=MESH
        )

    sends = {}

    def leaf_send(which, rho, col, dst_rho, dst_col, device):
        sends[LOSS, which] = remote((LOSS, which), loss_h.at[leaf(rho, col)], ext.at[4 * dst_rho + dst_col], device)
        sends[PLACE, which] = remote((PLACE, which), place_h.at[leaf(rho, col)], pext.at[4 * dst_rho + dst_col], device)

    for rho in (1, 2):
        leaf_send((LONP1, LONP2)[rho - 1], rho, 2, rho, 0, (lat, at_lon(1)))
        leaf_send((LONM1, LONM2)[rho - 1], rho, 1, rho, 3, (lat, at_lon(-1)))
    for b in (0, 1):
        leaf_send((PART0, PART1)[b], 2, 1 + b, 3, 1 + b, (partner, lon))
        leaf_send((CROSS0, CROSS1)[b], 1, 1 + b, 0, 1 + b, (cross, lon))
    leaf_send(XCP, 1, 2, 0, 0, (cross, at_lon(1)))
    leaf_send(XCM, 1, 1, 0, 3, (cross, at_lon(-1)))
    for k, col in ((0, 0), (1, 3)):
        for kind, ref in ((LOSS, ext), (PLACE, pext)):
            sends[kind, (FWD0, FWD1)[k]] = remote((kind, (FWD0, FWD1)[k]), ref.at[4 * 2 + col], ref.at[4 * 3 + col], (partner, lon))
    sends[LOSS, RELP] = remote((LOSS, RELP), ext.at[0], ext.at[4], (cross, lon))
    sends[LOSS, RELM] = remote((LOSS, RELM), ext.at[1], ext.at[7], (cross, at_lon(-1)))
    sends[COEF, RELP] = remote((COEF, RELP), coef.at[0], coef.at[3], (cross, lon))
    sends[COEF, RELM] = remote((COEF, RELM), coef.at[1], coef.at[5], (cross, at_lon(-1)))
    own = coef.at[4]
    sends[COEF, LONP] = remote((COEF, LONP), own, coef.at[3], (lat, at_lon(1)))
    sends[COEF, LONM] = remote((COEF, LONM), own, coef.at[5], (lat, at_lon(-1)))
    sends[COEF, PART] = remote((COEF, PART), own, coef.at[7], (partner, lon))
    sends[COEF, CROSS] = remote((COEF, CROSS), own, coef.at[1], (cross, lon))
    sends[COEF, XCP] = remote((COEF, XCP), own, coef.at[0], (cross, at_lon(1)))
    sends[COEF, XCM] = remote((COEF, XCM), own, coef.at[2], (cross, at_lon(-1)))
    sends[COEF, FWD0] = remote((COEF, FWD0), coef.at[3], coef.at[6], (partner, lon))
    sends[COEF, FWD1] = remote((COEF, FWD1), coef.at[5], coef.at[8], (partner, lon))
    for i, j in COLUMN:
        mine = cellw.at[1, hi, lat]
        sends[CELL, (i, j)] = remote((CELL, (i, j)), mine, mine, (lax.rem(lat + i, 4), lon + j * flip))
        theirs = cellw.at[1, lax.rem(hi + j, 2), lax.rem(lat + i, 4)]
        sends[CELLF, (i, j)] = remote((CELLF, (i, j)), theirs, theirs, (partner, lon))
    sends[CELL, PART] = remote((CELL, PART), cellw.at[1, hi, lat], cellw.at[1, hi, lat], (partner, lon))
    sends[WIN, 0] = remote((WIN, 0), cellw.at[1], cellw.at[2 * par], (lat, at_lon(2 * sign)))
    sends[WINF, 0] = remote((WINF, 0), cellw.at[2 * par], cellw.at[2 * par], (partner, lon))
    for m in FAR:
        sends[GROUP, m] = remote((GROUP, m), group, gall.at[m - 2], (lat, at_lon(2 * m)))
    sends[SUM, 0] = remote((SUM, 0), part.at[0], part.at[1], (partner, lon))

    def start(*names):
        for name in names:
            sends[name].start()

    def both(*whiches):
        return [(kind, which) for which in whiches for kind in (PLACE, LOSS)]

    def only(kind, *whiches):
        return [(kind, which) for which in whiches]

    def recv(*names):
        for name in names:
            sends[name].wait_recv()

    start(*only(PLACE, LONP2, LONM2, PART0, PART1, LONP1, LONM1))
    start(*only(LOSS, PART0, PART1, LONP2, LONM2))

    @pl.when(has_cross)
    def _():
        start(*only(PLACE, CROSS0, CROSS1, XCP, XCM))

    copies[BASIS].wait()
    for k, (rho, col) in enumerate(own_slots):
        copies[k].wait()
        l = leaf(rho, col)
        coef[4, l] = mm3(basis[l], ext[4 * rho + col])
    copies[LTRANS].wait()
    cellw[1, hi, lat] = mm3(ltrans[...].reshape(256, 64), coef[4].reshape(256, 256), ((0,), (0,)))
    start((CELL, PART), *[(CELL, pair) for pair in COLUMN])
    start((COEF, PART))

    @pl.when(has_cross)
    def _():
        start((COEF, XCP), (COEF, CROSS), (COEF, XCM))
        start(*only(LOSS, XCP, CROSS0, CROSS1, XCM))

    @pl.when(jnp.logical_not(has_cross))
    def _():
        start((COEF, LONP), (COEF, LONM))
        for k in range(3):
            coef[k] = jnp.zeros((4, 64, 256), f32)

    for c in place_copies:
        c.wait()

    for rho, col in own_slots:
        for axis in range(2):
            row = pext[4 * rho + col, axis : axis + 1, :] * UNIT
            columns[leaf(rho, col), axis] = jnp.transpose(jnp.broadcast_to(row, (128, 512)))

    def near_source(slot):
        def body(c, carry):
            rows = pl.ds(pl.multiple_of(c * 64, 64), 64)
            high, low = split(ext[slot, rows, :])
            sh[slot, rows, :] = high
            sl[slot, rows, :] = low
            return carry

        lax.fori_loop(0, 8, body, 0)

    def near_kernel(pair, half, high_ref, low_ref):
        rho_s, col_s, rho_t, col_t = pair
        di = (rho_s - rho_t) * sign
        dj = col_s - col_t
        l = leaf(rho_t, col_t)
        slot = 4 * rho_s + col_s
        off = (1 - flags[l // 2, l % 2, 3 * (di + 1) + dj + 1]).astype(f32) * AWAY
        src_row = (pext[slot, 0:1, :] + di.astype(f32)) * UNIT + off
        src_col = (pext[slot, 1:2, :] + dj.astype(f32)) * UNIT
        for c in range(4):
            rows = slice(64 * c, 64 * c + 64)
            for j in range(4):
                lanes = slice(128 * j, 128 * j + 128)
                dr = columns[l, 0, 256 * half + 64 * c : 256 * half + 64 * c + 64, :] - src_row[:, lanes]
                dc = columns[l, 1, 256 * half + 64 * c : 256 * half + 64 * c + 64, :] - src_col[:, lanes]
                sq = dr * dr + dc * dc
                d = sq * lax.rsqrt(jnp.maximum(sq, 1e-30))
                k = (1.0 + d) * jnp.exp2(d * -LOG2E)
                high, low = split(k)
                high_ref[rows, lanes] = high
                low_ref[rows, lanes] = low

    def near_product(pair, half, high_ref, low_ref):
        rho_s, col_s, rho_t, col_t = pair
        l = leaf(rho_t, col_t)
        slot = 4 * rho_s + col_s
        high = high_ref[...]
        source = sh[slot]
        acc[l, 256 * half : 256 * half + 256, :] += mm(high, source) + mm(low_ref[...], source) + mm(high, sl[slot])

    def near(count, pair_of):
        def typed(i):
            return tuple(jnp.asarray(v, jnp.int32) for v in pair_of(i))

        near_kernel(typed(jnp.int32(0)), 0, ka_h, ka_l)

        def body(i, carry):
            pair = typed(i)
            near_kernel(pair, 1, kb_h, kb_l)
            near_product(pair, 0, ka_h, ka_l)
            near_kernel(typed(jnp.minimum(i + 1, count - 1)), 0, ka_h, ka_l)
            near_product(pair, 1, kb_h, kb_l)
            return carry

        lax.fori_loop(0, count, body, 0)

    def split_all(*slots):
        for slot in slots:
            near_source(slot)

    for k, (rho, col) in enumerate(own_slots):
        acc[leaf(rho, col)] = 0.5 * ext[4 * rho + col]
    split_all(5, 6, 9, 10)
    near(16, lambda i: (1 + i // 8, 1 + (i // 4) % 2, 1 + (i // 2) % 2, 1 + i % 2))
    recv(*[(CELL, pair) for pair in COLUMN])
    start(*[(CELLF, pair) for pair in COLUMN])
    recv(*both(PART0, PART1))
    split_all(13, 14)
    near(4, lambda i: (3, 1 + i // 2, 2, 1 + i % 2))

    copies[DTRANS].wait()
    recv((CELL, PART), *[(CELLF, pair) for pair in COLUMN])
    start((WIN, 0))
    first = 2 * par
    total = jnp.zeros((64, 256), f32)
    for f in range(2):
        for e in range(2):
            total += mm3(dtrans[first + e, f], cellw[1, f, first + e], ((0,), (0,)))
    group[...] = total
    start(*[(GROUP, m) for m in FAR])
    @pl.when(jnp.logical_not(has_cross))
    def _():
        start(*only(LOSS, LONP1, LONM1))

    @pl.when(has_cross)
    def _():
        recv((COEF, XCP), (COEF, CROSS))
        start((COEF, RELP), (COEF, RELM))

    recv(*both(LONP2, LONM2))
    start(*both(FWD0, FWD1))
    split_all(8, 11)
    near(4, lambda i: (2, 3 * (i // 2), 1 + i % 2, 1 + i // 2))

    @pl.when(has_cross)
    def _():
        recv(*both(XCP, CROSS0))
        start((LOSS, RELP), (LOSS, RELM))
        recv(*both(CROSS1, XCM), (COEF, RELP), (COEF, RELM))

    @pl.when(jnp.logical_not(has_cross))
    def _():
        recv((COEF, LONP), (COEF, LONM))

    start((COEF, FWD0), (COEF, FWD1))
    recv((WIN, 0))
    start((WINF, 0))

    @pl.when(has_cross)
    def _():
        split_all(0, 1, 2, 3)
        near(6, lambda i: (0, (i + 1) // 2, 1, jnp.where(i % 2 == 1, jnp.maximum(1, (i - 1) // 2), jnp.minimum(2, i // 2 + 1))))

    recv(*both(FWD0, FWD1))
    split_all(12, 15)
    near(2, lambda i: (3, 3 * i, 2, 1 + i))

    copies[DCOUP].wait()
    copies[GCOUP].wait()
    copies[LCOUP].wait()
    recv((COEF, PART), (COEF, FWD0), (COEF, FWD1))

    @pl.when(has_cross)
    def _():
        recv((COEF, XCM))

    field[...] = jnp.zeros((256, 256), f32)

    def leaf_body(i, carry):
        side, v_side = i // 3, i % 3
        slot = 3 * (side + par * (2 - 2 * side)) + v_side
        total = field[...]
        for a in range(2):
            for b in range(2):
                u, v = 2 * side + a, 2 * v_side + b
                w = 6 * u + v
                weights = []
                for l in range(4):
                    di, dj = u - 2 - l // 2, v - 2 - l % 2
                    inside = (jnp.abs(di) <= 1) & (jnp.abs(dj) <= 1)
                    index = 3 * (jnp.clip(di, -1, 1) + 1) + jnp.clip(dj, -1, 1) + 1
                    keep = (1 - flags[l // 2, l % 2, index] * jnp.where(inside, 1, 0)).astype(f32)
                    weights.append((lcoup[l, w].astype(f32) * keep).astype(bf16))
                total += mm2(jnp.concatenate(weights, 0), coef[slot, 2 * a + b])
        field[...] = total
        return carry

    lax.fori_loop(0, 9, leaf_body, 0)
    recv((WINF, 0))

    def window_body(v, total):
        hoff, f = v // 2, v % 2
        for row in range(4):
            w = 6 * (row + 2 - 2 * row_group) + v
            away = (jnp.abs(row - lat) > 1) | (jnp.abs(v - 2 - hi) > 1)
            keep = jnp.where(away, 1.0, 0.0)
            weight = (dcoup[w].astype(f32) * keep).astype(bf16)
            total += mm2(weight, cellw[hoff, f, row])
        return total

    device_far = lax.fori_loop(0, 6, window_body, jnp.zeros((64, 256), f32))
    recv(*[(GROUP, m) for m in FAR])
    total = jnp.zeros((64, 256), f32)
    for m in FAR:
        total += mm2(gcoup[lax.rem(col_group - m + 16, 16)], gall[m - 2])
    part[0] = total
    start((SUM, 0))
    recv((SUM, 0))
    device_field = device_far + mm3(dtrans[lat, hi], part[0] + part[1])
    field[...] += mm3(ltrans[...].reshape(256, 64), device_field)
    for l in range(4):
        acc[l] += mm3(basis[l], field[pl.ds(64 * l, 64), :], ((0,), (0,)))

    @pl.when(jnp.logical_not(has_cross))
    def _():
        recv(*only(LOSS, LONP1, LONM1))

    @pl.when(has_cross)
    def _():
        recv(*only(LOSS, RELP, RELM))

    recv(*only(PLACE, LONP1, LONM1))
    split_all(4, 7)
    near(4, lambda i: (1, 3 * (i // 2), 1 + i % 2, 1 + i // 2))

    crossing = [(COEF, w) for w in (CROSS, XCP, XCM, RELP, RELM)] + both(CROSS0, CROSS1, XCP, XCM)
    crossing += only(LOSS, RELP, RELM)
    direct = [(COEF, LONP), (COEF, LONM)] + only(LOSS, LONP1, LONM1)
    for name in sends:
        if name not in crossing and name not in direct:
            sends[name].wait_send()

    @pl.when(has_cross)
    def _():
        for name in crossing:
            sends[name].wait_send()

    @pl.when(jnp.logical_not(has_cross))
    def _():
        for name in direct:
            sends[name].wait_send()


def local(losses, positions, leaf_basis, near_flags, leaf_coupling, leaf_transfer, device_coupling, device_transfer, group_coupling):
    anywhere = pl.BlockSpec(memory_space=pl.ANY)
    vmem = pltpu.VMEM
    call = pl.pallas_call(
        kernel,
        out_shape=jax.ShapeDtypeStruct((4, 512, 256), f32),
        in_specs=[anywhere, anywhere, pl.BlockSpec(memory_space=pltpu.SMEM)] + [anywhere] * 6,
        out_specs=pl.BlockSpec(memory_space=pltpu.VMEM),
        scratch_shapes=[
            vmem((16, 512, 256), f32), vmem((16, 2, 512), f32), vmem((9, 4, 64, 256), f32),
            vmem((3, 2, 4, 64, 256), f32), vmem((64, 256), f32), vmem((13, 64, 256), f32), vmem((2, 64, 256), f32),
            vmem((256, 512), bf16), vmem((256, 512), bf16),
            vmem((256, 512), bf16), vmem((256, 512), bf16),
            vmem((16, 512, 256), bf16), vmem((16, 512, 256), bf16), vmem((256, 256), f32), vmem((4, 2, 512, 128), f32),
            vmem((4, 64, 512), f32), vmem((4, 36, 64, 64), bf16), vmem((4, 64, 64), f32),
            vmem((36, 64, 64), bf16), vmem((4, 2, 64, 64), f32), vmem((16, 64, 64), bf16),
            pltpu.SemaphoreType.DMA((14,)),
            pltpu.SemaphoreType.DMA((len(SEMS),)), pltpu.SemaphoreType.DMA((len(SEMS),)),
        ],
        compiler_params=pltpu.CompilerParams(collective_id=0, has_side_effects=True, vmem_limit_bytes=40 * 1024 * 1024),
        name="apply",
    )
    hbm = lambda x: pltpu.with_memory_space_constraint(x, pltpu.HBM)
    out = call(
        hbm(losses.reshape(4, 512, 256)), hbm(positions.reshape(4, 2, 512)), near_flags,
        hbm(jnp.swapaxes(leaf_basis, 2, 3).reshape(4, 64, 512)), hbm(leaf_coupling.reshape(4, 36, 64, 64)),
        hbm(leaf_transfer.reshape(4, 64, 64)), hbm(device_coupling.reshape(36, 64, 64)), hbm(device_transfer), hbm(group_coupling),
    )
    return out.reshape(2, 2, 512, 256)


def solution(mesh):
    placed = (
        P("lat", "lon", None, None),
        P("lat", "lon", None, None),
        P("lat", "lon", None, None),
        P("lat", "lon", None),
        P("lat", "lon", None, None, None),
        P("lat", "lon", None, None),
        P("lat", "lon", None, None, None),
        P(),
        P(),
    )
    return jax.shard_map(
        local, mesh=mesh, in_specs=placed, out_specs=P("lat", "lon", None, None), check_vma=False
    )
```

```python
import jax
import jax.numpy as jnp
from jax import lax
from jax.experimental import pallas as pl
from jax.experimental.pallas import tpu as pltpu
from jax.sharding import PartitionSpec as P

MESH = pl.DeviceIdType.MESH
LOG2E = 1.4426950408889634
UNIT = 1.7320508075688772 / 0.15
AWAY = 1.0e4
f32, bf16 = jnp.float32, jnp.bfloat16


LOSS, PLACE, COEF, CELL, CELLF, WIN, WINF, GROUP, SUM = range(9)
LONP, LONM, LONP1, LONP2, LONM1, LONM2, PART, PART0, PART1, CROSS, CROSS0, CROSS1, XCP, XCM, FWD0, FWD1, RELP, RELM = range(18)
BASIS, LCOUP, LTRANS, DCOUP, DTRANS, GCOUP = range(10, 16)


def split(x):
    high = x.astype(bf16)
    return high, (x - high.astype(f32)).astype(bf16)


def mm(a, b, dims=((1,), (0,))):
    return lax.dot_general(a, b, (dims, ((), ())), preferred_element_type=f32)


def mm3(a, b, dims=((1,), (0,))):
    ah, al = split(a)
    bh, bl = split(b)
    return mm(ah, bh, dims) + mm(al, bh, dims) + mm(ah, bl, dims)


def mm2(a, b):
    bh, bl = split(b)
    return mm(a, bh) + mm(a, bl)


FAR = tuple(range(2, 15))
COLUMN = ((2, 0), (0, 1), (2, 1))


def remote_names():
    names = []
    for kind in (LOSS, PLACE):
        for which in (LONP1, LONP2, LONM1, LONM2, PART0, PART1, CROSS0, CROSS1, XCP, XCM, FWD0, FWD1, RELP, RELM):
            names.append((kind, which))
    for which in (LONP, LONM, PART, CROSS, XCP, XCM, FWD0, FWD1, RELP, RELM):
        names.append((COEF, which))
    for pair in COLUMN:
        names += [(CELL, pair), (CELLF, pair)]
    names += [(CELL, PART), (WIN, 0), (WINF, 0), (SUM, 0)]
    for m in FAR:
        names.append((GROUP, m))
    return {name: k for k, name in enumerate(names)}


SEMS = remote_names()


def kernel(
    loss_h, place_h, flags, basis_h, lcoup_h, ltrans_h, dcoup_h, dtrans_h, gcoup_h,
    acc,
    ext, pext, coef, cellw, group, gall, part, ka_h, ka_l, kb_h, kb_l, sh, sl, field, columns, kw_h, kw_l,
    basis, lcoup, ltrans, dcoup, dtrans, gcoup,
    lsem, ssem, rsem,
):
    lat, lon = lax.axis_index("lat"), lax.axis_index("lon")
    n_lon = lax.axis_size("lon")
    par, hi = lax.rem(lat, 2), lax.rem(lon, 2)
    row_group, col_group = lat // 2, lon // 2
    sign = 1 - 2 * par
    has_cross = (lat == 1) | (lat == 2)
    partner, cross = lat + sign, lat - sign

    def leaf(rho, col):
        return 2 * (par + (rho - 1) * sign) + (col - 1)

    def at_lon(step):
        return lax.rem(lon + step + n_lon, n_lon)

    def local(src, dst, k):
        return pltpu.make_async_copy(src, dst, lsem.at[k])

    own_slots = [(1, 1), (1, 2), (2, 1), (2, 2)]
    copies = {}
    for k, (rho, col) in enumerate(own_slots):
        copies[k] = local(loss_h.at[leaf(rho, col)], ext.at[4 * rho + col], k)
    for k, (src, dst, name) in enumerate((
        (basis_h, basis, BASIS), (lcoup_h, lcoup, LCOUP), (ltrans_h, ltrans, LTRANS),
        (dcoup_h, dcoup, DCOUP), (dtrans_h.at[:, pl.ds(2 * col_group, 2)], dtrans, DTRANS),
        (gcoup_h.at[row_group, col_group, par], gcoup, GCOUP),
    )):
        copies[name] = local(src, dst, 4 + k)
    place_copies = [
        local(place_h.at[leaf(rho, col)], pext.at[4 * rho + col], 10 + k) for k, (rho, col) in enumerate(own_slots)
    ]
    for k in range(4):
        copies[k].start()
    for name in (BASIS, LTRANS):
        copies[name].start()
    for c in place_copies:
        c.start()
    for name in (DTRANS, LCOUP, DCOUP, GCOUP):
        copies[name].start()

    barrier = pltpu.get_barrier_semaphore()

    def hello(a, b):
        pl.semaphore_signal(barrier, inc=1, device_id=(a, b), device_id_type=MESH)

    flip = 1 - 2 * hi
    for i, j in COLUMN:
        hello(lax.rem(lat + i, 4), lon + j * flip)
    hello(partner, lon)
    for m in range(1, 16):
        hello(lat, at_lon(2 * m))
    hello(lat, at_lon(1))
    hello(lat, at_lon(-1))

    @pl.when(has_cross)
    def _():
        hello(cross, lon)
        hello(cross, at_lon(1))
        hello(cross, at_lon(-1))

    pl.semaphore_wait(barrier, 4 + 15 + 2 + jnp.where(has_cross, 3, 0).astype(jnp.int32))

    def remote(name, src, dst, device):
        k = SEMS[name]
        return pltpu.make_async_remote_copy(
            src_ref=src, dst_ref=dst, send_sem=ssem.at[k], recv_sem=rsem.at[k], device_id=device, device_id_type=MESH
        )

    sends = {}

    def leaf_send(which, rho, col, dst_rho, dst_col, device):
        sends[LOSS, which] = remote((LOSS, which), loss_h.at[leaf(rho, col)], ext.at[4 * dst_rho + dst_col], device)
        sends[PLACE, which] = remote((PLACE, which), place_h.at[leaf(rho, col)], pext.at[4 * dst_rho + dst_col], device)

    for rho in (1, 2):
        leaf_send((LONP1, LONP2)[rho - 1], rho, 2, rho, 0, (lat, at_lon(1)))
        leaf_send((LONM1, LONM2)[rho - 1], rho, 1, rho, 3, (lat, at_lon(-1)))
    for b in (0, 1):
        leaf_send((PART0, PART1)[b], 2, 1 + b, 3, 1 + b, (partner, lon))
        leaf_send((CROSS0, CROSS1)[b], 1, 1 + b, 0, 1 + b, (cross, lon))
    leaf_send(XCP, 1, 2, 0, 0, (cross, at_lon(1)))
    leaf_send(XCM, 1, 1, 0, 3, (cross, at_lon(-1)))
    for k, col in ((0, 0), (1, 3)):
        for kind, ref in ((LOSS, ext), (PLACE, pext)):
            sends[kind, (FWD0, FWD1)[k]] = remote((kind, (FWD0, FWD1)[k]), ref.at[4 * 2 + col], ref.at[4 * 3 + col], (partner, lon))
    sends[LOSS, RELP] = remote((LOSS, RELP), ext.at[0], ext.at[4], (cross, lon))
    sends[LOSS, RELM] = remote((LOSS, RELM), ext.at[1], ext.at[7], (cross, at_lon(-1)))
    sends[COEF, RELP] = remote((COEF, RELP), coef.at[0], coef.at[3], (cross, lon))
    sends[COEF, RELM] = remote((COEF, RELM), coef.at[1], coef.at[5], (cross, at_lon(-1)))
    own = coef.at[4]
    sends[COEF, LONP] = remote((COEF, LONP), own, coef.at[3], (lat, at_lon(1)))
    sends[COEF, LONM] = remote((COEF, LONM), own, coef.at[5], (lat, at_lon(-1)))
    sends[COEF, PART] = remote((COEF, PART), own, coef.at[7], (partner, lon))
    sends[COEF, CROSS] = remote((COEF, CROSS), own, coef.at[1], (cross, lon))
    sends[COEF, XCP] = remote((COEF, XCP), own, coef.at[0], (cross, at_lon(1)))
    sends[COEF, XCM] = remote((COEF, XCM), own, coef.at[2], (cross, at_lon(-1)))
    sends[COEF, FWD0] = remote((COEF, FWD0), coef.at[3], coef.at[6], (partner, lon))
    sends[COEF, FWD1] = remote((COEF, FWD1), coef.at[5], coef.at[8], (partner, lon))
    for i, j in COLUMN:
        mine = cellw.at[1, hi, lat]
        sends[CELL, (i, j)] = remote((CELL, (i, j)), mine, mine, (lax.rem(lat + i, 4), lon + j * flip))
        theirs = cellw.at[1, lax.rem(hi + j, 2), lax.rem(lat + i, 4)]
        sends[CELLF, (i, j)] = remote((CELLF, (i, j)), theirs, theirs, (partner, lon))
    sends[CELL, PART] = remote((CELL, PART), cellw.at[1, hi, lat], cellw.at[1, hi, lat], (partner, lon))
    sends[WIN, 0] = remote((WIN, 0), cellw.at[1], cellw.at[2 * par], (lat, at_lon(2 * sign)))
    sends[WINF, 0] = remote((WINF, 0), cellw.at[2 * par], cellw.at[2 * par], (partner, lon))
    for m in FAR:
        sends[GROUP, m] = remote((GROUP, m), group, gall.at[m - 2], (lat, at_lon(2 * m)))
    sends[SUM, 0] = remote((SUM, 0), part.at[0], part.at[1], (partner, lon))

    def start(*names):
        for name in names:
            sends[name].start()

    def both(*whiches):
        return [(kind, which) for which in whiches for kind in (PLACE, LOSS)]

    def only(kind, *whiches):
        return [(kind, which) for which in whiches]

    def recv(*names):
        for name in names:
            sends[name].wait_recv()

    start(*only(PLACE, LONP2, LONM2, PART0, PART1, LONP1, LONM1))
    start(*only(LOSS, PART0, PART1, LONP2, LONM2))

    @pl.when(has_cross)
    def _():
        start(*only(PLACE, CROSS0, CROSS1, XCP, XCM))

    copies[BASIS].wait()
    for k, (rho, col) in enumerate(own_slots):
        copies[k].wait()
        l = leaf(rho, col)
        coef[4, l] = mm3(basis[l], ext[4 * rho + col])
    copies[LTRANS].wait()
    cellw[1, hi, lat] = mm3(ltrans[...].reshape(256, 64), coef[4].reshape(256, 256), ((0,), (0,)))
    start((CELL, PART), *[(CELL, pair) for pair in COLUMN])
    start((COEF, PART))

    @pl.when(has_cross)
    def _():
        start((COEF, XCP), (COEF, CROSS), (COEF, XCM))
        start(*only(LOSS, XCP, CROSS0, CROSS1, XCM))

    @pl.when(jnp.logical_not(has_cross))
    def _():
        start((COEF, LONP), (COEF, LONM))
        start(*only(LOSS, LONP1, LONM1))
        for k in range(3):
            coef[k] = jnp.zeros((4, 64, 256), f32)

    for c in place_copies:
        c.wait()

    for rho, col in own_slots:
        for axis in range(2):
            row = pext[4 * rho + col, axis : axis + 1, :] * UNIT
            columns[leaf(rho, col), axis] = jnp.transpose(jnp.broadcast_to(row, (128, 512)))

    def near_source(slot):
        def body(c, carry):
            rows = pl.ds(pl.multiple_of(c * 64, 64), 64)
            high, low = split(ext[slot, rows, :])
            sh[slot, rows, :] = high
            sl[slot, rows, :] = low
            return carry

        lax.fori_loop(0, 8, body, 0)

    def near_kernel(pair, half, high_ref, low_ref):
        rho_s, col_s, rho_t, col_t = pair
        di = (rho_s - rho_t) * sign
        dj = col_s - col_t
        l = leaf(rho_t, col_t)
        slot = 4 * rho_s + col_s
        off = (1 - flags[l // 2, l % 2, 3 * (di + 1) + dj + 1]).astype(f32) * AWAY
        src_row = (pext[slot, 0:1, :] + di.astype(f32)) * UNIT + off
        src_col = (pext[slot, 1:2, :] + dj.astype(f32)) * UNIT
        for c in range(4):
            rows = slice(64 * c, 64 * c + 64)
            for j in range(4):
                lanes = slice(128 * j, 128 * j + 128)
                dr = columns[l, 0, 256 * half + 64 * c : 256 * half + 64 * c + 64, :] - src_row[:, lanes]
                dc = columns[l, 1, 256 * half + 64 * c : 256 * half + 64 * c + 64, :] - src_col[:, lanes]
                sq = dr * dr + dc * dc
                d = sq * lax.rsqrt(jnp.maximum(sq, 1e-30))
                k = (1.0 + d) * jnp.exp2(d * -LOG2E)
                high, low = split(k)
                high_ref[rows, lanes] = high
                low_ref[rows, lanes] = low

    def near_product(pair, half, high_ref, low_ref):
        rho_s, col_s, rho_t, col_t = pair
        l = leaf(rho_t, col_t)
        slot = 4 * rho_s + col_s
        high = high_ref[...]
        source = sh[slot]
        acc[l, 256 * half : 256 * half + 256, :] += mm(high, source) + mm(low_ref[...], source) + mm(high, sl[slot])

    def near(count, pair_of):
        def typed(i):
            return tuple(jnp.asarray(v, jnp.int32) for v in pair_of(i))

        near_kernel(typed(jnp.int32(0)), 0, ka_h, ka_l)

        def body(i, carry):
            pair = typed(i)
            near_kernel(pair, 1, kb_h, kb_l)
            near_product(pair, 0, ka_h, ka_l)
            near_kernel(typed(jnp.minimum(i + 1, count - 1)), 0, ka_h, ka_l)
            near_product(pair, 1, kb_h, kb_l)
            return carry

        lax.fori_loop(0, count, body, 0)

    def split_all(*slots):
        for slot in slots:
            near_source(slot)

    for k, (rho, col) in enumerate(own_slots):
        acc[leaf(rho, col)] = 0.5 * ext[4 * rho + col]
    split_all(5, 6, 9, 10)
    near(16, lambda i: (1 + i // 8, 1 + (i // 4) % 2, 1 + (i // 2) % 2, 1 + i % 2))
    recv(*[(CELL, pair) for pair in COLUMN])
    start(*[(CELLF, pair) for pair in COLUMN])
    recv(*both(PART0, PART1))
    split_all(13, 14)
    near(4, lambda i: (3, 1 + i // 2, 2, 1 + i % 2))

    copies[DTRANS].wait()
    recv((CELL, PART), *[(CELLF, pair) for pair in COLUMN])
    start((WIN, 0))
    first = 2 * par
    total = jnp.zeros((64, 256), f32)
    for f in range(2):
        for e in range(2):
            total += mm3(dtrans[first + e, f], cellw[1, f, first + e], ((0,), (0,)))
    group[...] = total
    start(*[(GROUP, m) for m in FAR])
    @pl.when(has_cross)
    def _():
        recv((COEF, XCP), (COEF, CROSS))
        start((COEF, RELP), (COEF, RELM))

    recv(*both(LONP2, LONM2))
    start(*both(FWD0, FWD1))
    split_all(8, 11)
    near(4, lambda i: (2, 3 * (i // 2), 1 + i % 2, 1 + i // 2))

    @pl.when(has_cross)
    def _():
        recv(*both(XCP, CROSS0))
        start((LOSS, RELP), (LOSS, RELM))
        recv(*both(CROSS1, XCM), (COEF, RELP), (COEF, RELM))

    @pl.when(jnp.logical_not(has_cross))
    def _():
        recv((COEF, LONP), (COEF, LONM))

    start((COEF, FWD0), (COEF, FWD1))
    recv((WIN, 0))
    start((WINF, 0))

    @pl.when(has_cross)
    def _():
        split_all(0, 1, 2, 3)
        near(6, lambda i: (0, (i + 1) // 2, 1, jnp.where(i % 2 == 1, jnp.maximum(1, (i - 1) // 2), jnp.minimum(2, i // 2 + 1))))

    recv(*both(FWD0, FWD1))
    split_all(12, 15)
    near(2, lambda i: (3, 3 * i, 2, 1 + i))

    copies[DCOUP].wait()
    copies[GCOUP].wait()
    copies[LCOUP].wait()
    recv((COEF, PART), (COEF, FWD0), (COEF, FWD1))

    @pl.when(has_cross)
    def _():
        recv((COEF, XCM))

    field[...] = jnp.zeros((256, 256), f32)

    def leaf_body(i, carry):
        side, v_side = i // 3, i % 3
        slot = 3 * (side + par * (2 - 2 * side)) + v_side
        total = field[...]
        for a in range(2):
            for b in range(2):
                u, v = 2 * side + a, 2 * v_side + b
                w = 6 * u + v
                weights = []
                for l in range(4):
                    di, dj = u - 2 - l // 2, v - 2 - l % 2
                    inside = (jnp.abs(di) <= 1) & (jnp.abs(dj) <= 1)
                    index = 3 * (jnp.clip(di, -1, 1) + 1) + jnp.clip(dj, -1, 1) + 1
                    keep = (1 - flags[l // 2, l % 2, index] * jnp.where(inside, 1, 0)).astype(f32)
                    weights.append((lcoup[l, w].astype(f32) * keep).astype(bf16))
                total += mm2(jnp.concatenate(weights, 0), coef[slot, 2 * a + b])
        field[...] = total
        return carry

    lax.fori_loop(0, 9, leaf_body, 0)

    def last(side, t):
        return (jnp.int32(1), jnp.int32(3 * side), jnp.asarray(1 + t, jnp.int32), jnp.int32(1 + side))

    def halves(side, t, fn):
        for half in range(2):
            rows = pl.ds(256 * half, 256)
            fn(last(side, t), half, kw_h.at[2 * side + t, rows], kw_l.at[2 * side + t, rows])

    recv(*only(PLACE, LONP1, LONM1))
    for side in range(2):

        def prepare(t, carry, side=side):
            halves(side, t, near_kernel)
            return carry

        lax.fori_loop(0, 2, prepare, 0)

    recv((WINF, 0))

    def window_body(v, total):
        hoff, f = v // 2, v % 2
        for row in range(4):
            w = 6 * (row + 2 - 2 * row_group) + v
            away = (jnp.abs(row - lat) > 1) | (jnp.abs(v - 2 - hi) > 1)
            keep = jnp.where(away, 1.0, 0.0)
            weight = (dcoup[w].astype(f32) * keep).astype(bf16)
            total += mm2(weight, cellw[hoff, f, row])
        return total

    device_far = lax.fori_loop(0, 6, window_body, jnp.zeros((64, 256), f32))
    recv(*[(GROUP, m) for m in FAR])
    total = jnp.zeros((64, 256), f32)
    for m in FAR:
        total += mm2(gcoup[lax.rem(col_group - m + 16, 16)], gall[m - 2])
    part[0] = total
    start((SUM, 0))
    recv((SUM, 0))
    device_field = device_far + mm3(dtrans[lat, hi], part[0] + part[1])
    field[...] += mm3(ltrans[...].reshape(256, 64), device_field)
    for l in range(4):
        acc[l] += mm3(basis[l], field[pl.ds(64 * l, 64), :], ((0,), (0,)))

    for side, straight, relayed in ((0, LONP1, RELP), (1, LONM1, RELM)):

        @pl.when(jnp.logical_not(has_cross))
        def _():
            recv((LOSS, straight))

        @pl.when(has_cross)
        def _():
            recv((LOSS, relayed))

        split_all(4 + 3 * side)

        def finish(t, carry, side=side):
            halves(side, t, near_product)
            return carry

        lax.fori_loop(0, 2, finish, 0)

    crossing = [(COEF, w) for w in (CROSS, XCP, XCM, RELP, RELM)] + both(CROSS0, CROSS1, XCP, XCM)
    crossing += only(LOSS, RELP, RELM)
    direct = [(COEF, LONP), (COEF, LONM)] + only(LOSS, LONP1, LONM1)
    for name in sends:
        if name not in crossing and name not in direct:
            sends[name].wait_send()

    @pl.when(has_cross)
    def _():
        for name in crossing:
            sends[name].wait_send()

    @pl.when(jnp.logical_not(has_cross))
    def _():
        for name in direct:
            sends[name].wait_send()


def local(losses, positions, leaf_basis, near_flags, leaf_coupling, leaf_transfer, device_coupling, device_transfer, group_coupling):
    anywhere = pl.BlockSpec(memory_space=pl.ANY)
    vmem = pltpu.VMEM
    call = pl.pallas_call(
        kernel,
        out_shape=jax.ShapeDtypeStruct((4, 512, 256), f32),
        in_specs=[anywhere, anywhere, pl.BlockSpec(memory_space=pltpu.SMEM)] + [anywhere] * 6,
        out_specs=pl.BlockSpec(memory_space=pltpu.VMEM),
        scratch_shapes=[
            vmem((16, 512, 256), f32), vmem((16, 2, 512), f32), vmem((9, 4, 64, 256), f32),
            vmem((3, 2, 4, 64, 256), f32), vmem((64, 256), f32), vmem((13, 64, 256), f32), vmem((2, 64, 256), f32),
            vmem((256, 512), bf16), vmem((256, 512), bf16),
            vmem((256, 512), bf16), vmem((256, 512), bf16),
            vmem((16, 512, 256), bf16), vmem((16, 512, 256), bf16), vmem((256, 256), f32), vmem((4, 2, 512, 128), f32),
            vmem((4, 512, 512), bf16), vmem((4, 512, 512), bf16),
            vmem((4, 64, 512), f32), vmem((4, 36, 64, 64), bf16), vmem((4, 64, 64), f32),
            vmem((36, 64, 64), bf16), vmem((4, 2, 64, 64), f32), vmem((16, 64, 64), bf16),
            pltpu.SemaphoreType.DMA((14,)),
            pltpu.SemaphoreType.DMA((len(SEMS),)), pltpu.SemaphoreType.DMA((len(SEMS),)),
        ],
        compiler_params=pltpu.CompilerParams(collective_id=0, has_side_effects=True, vmem_limit_bytes=40 * 1024 * 1024),
        name="apply",
    )
    hbm = lambda x: pltpu.with_memory_space_constraint(x, pltpu.HBM)
    out = call(
        hbm(losses.reshape(4, 512, 256)), hbm(positions.reshape(4, 2, 512)), near_flags,
        hbm(jnp.swapaxes(leaf_basis, 2, 3).reshape(4, 64, 512)), hbm(leaf_coupling.reshape(4, 36, 64, 64)),
        hbm(leaf_transfer.reshape(4, 64, 64)), hbm(device_coupling.reshape(36, 64, 64)), hbm(device_transfer), hbm(group_coupling),
    )
    return out.reshape(2, 2, 512, 256)


def solution(mesh):
    placed = (
        P("lat", "lon", None, None),
        P("lat", "lon", None, None),
        P("lat", "lon", None, None),
        P("lat", "lon", None),
        P("lat", "lon", None, None, None),
        P("lat", "lon", None, None),
        P("lat", "lon", None, None, None),
        P(),
        P(),
    )
    return jax.shard_map(
        local, mesh=mesh, in_specs=placed, out_specs=P("lat", "lon", None, None), check_vma=False
    )
```

```python
import jax
import jax.numpy as jnp
from jax import lax
from jax.experimental import pallas as pl
from jax.experimental.pallas import tpu as pltpu
from jax.sharding import PartitionSpec as P

MESH = pl.DeviceIdType.MESH
LOG2E = 1.4426950408889634
UNIT = 1.7320508075688772 / 0.15
AWAY = 1.0e4
f32, bf16 = jnp.float32, jnp.bfloat16


LOSS, PLACE, COEF, CELL, CELLF, WIN, WINF, GROUP, SUM = range(9)
LONP, LONM, LONP1, LONP2, LONM1, LONM2, PART, PART0, PART1, CROSS, CROSS0, CROSS1, XCP, XCM, FWD0, FWD1, RELP, RELM = range(18)
BASIS, LCOUP, LTRANS, DCOUP, DTRANS, GCOUP = range(10, 16)


def split(x):
    high = x.astype(bf16)
    return high, (x - high.astype(f32)).astype(bf16)


def mm(a, b, dims=((1,), (0,))):
    return lax.dot_general(a, b, (dims, ((), ())), preferred_element_type=f32)


def mm3(a, b, dims=((1,), (0,))):
    ah, al = split(a)
    bh, bl = split(b)
    return mm(ah, bh, dims) + mm(al, bh, dims) + mm(ah, bl, dims)


def mm2(a, b):
    bh, bl = split(b)
    return mm(a, bh) + mm(a, bl)


FAR = tuple(range(2, 15))
COLUMN = ((2, 0), (0, 1), (2, 1))


def remote_names():
    names = []
    for kind in (LOSS, PLACE):
        for which in (LONP1, LONP2, LONM1, LONM2, PART0, PART1, CROSS0, CROSS1, XCP, XCM, FWD0, FWD1, RELP, RELM):
            names.append((kind, which))
    for which in (LONP, LONM, PART, CROSS, XCP, XCM, FWD0, FWD1, RELP, RELM):
        names.append((COEF, which))
    for pair in COLUMN:
        names += [(CELL, pair), (CELLF, pair)]
    names += [(CELL, PART), (WIN, 0), (WINF, 0), (SUM, 0)]
    for m in FAR:
        names.append((GROUP, m))
    return {name: k for k, name in enumerate(names)}


SEMS = remote_names()


def kernel(
    loss_h, place_h, flags, basis_h, lcoup_h, ltrans_h, dcoup_h, dtrans_h, gcoup_h,
    acc,
    ext, pext, coef, cellw, group, gall, part, ka_h, ka_l, kb_h, kb_l, sh, sl, field, columns, kw_h, kw_l,
    basis, lcoup, ltrans, dcoup, dtrans, gcoup,
    lsem, ssem, rsem,
):
    lat, lon = lax.axis_index("lat"), lax.axis_index("lon")
    n_lon = lax.axis_size("lon")
    par, hi = lax.rem(lat, 2), lax.rem(lon, 2)
    row_group, col_group = lat // 2, lon // 2
    sign = 1 - 2 * par
    has_cross = (lat == 1) | (lat == 2)
    partner, cross = lat + sign, lat - sign

    def leaf(rho, col):
        return 2 * (par + (rho - 1) * sign) + (col - 1)

    def at_lon(step):
        return lax.rem(lon + step + n_lon, n_lon)

    def local(src, dst, k):
        return pltpu.make_async_copy(src, dst, lsem.at[k])

    own_slots = [(1, 1), (1, 2), (2, 1), (2, 2)]
    copies = {}
    for k, (rho, col) in enumerate(own_slots):
        copies[k] = local(loss_h.at[leaf(rho, col)], ext.at[4 * rho + col], k)
    for k, (src, dst, name) in enumerate((
        (basis_h, basis, BASIS), (lcoup_h, lcoup, LCOUP), (ltrans_h, ltrans, LTRANS),
        (dcoup_h, dcoup, DCOUP), (dtrans_h.at[:, pl.ds(2 * col_group, 2)], dtrans, DTRANS),
        (gcoup_h.at[row_group, col_group, par], gcoup, GCOUP),
    )):
        copies[name] = local(src, dst, 4 + k)
    place_copies = [
        local(place_h.at[leaf(rho, col)], pext.at[4 * rho + col], 10 + k) for k, (rho, col) in enumerate(own_slots)
    ]
    for k in range(4):
        copies[k].start()
    for name in (BASIS, LTRANS):
        copies[name].start()
    for c in place_copies:
        c.start()
    for name in (DTRANS, LCOUP, DCOUP, GCOUP):
        copies[name].start()

    barrier = pltpu.get_barrier_semaphore()

    def hello(a, b):
        pl.semaphore_signal(barrier, inc=1, device_id=(a, b), device_id_type=MESH)

    flip = 1 - 2 * hi
    for i, j in COLUMN:
        hello(lax.rem(lat + i, 4), lon + j * flip)
    hello(partner, lon)
    for m in range(1, 16):
        hello(lat, at_lon(2 * m))
    hello(lat, at_lon(1))
    hello(lat, at_lon(-1))

    @pl.when(has_cross)
    def _():
        hello(cross, lon)
        hello(cross, at_lon(1))
        hello(cross, at_lon(-1))

    pl.semaphore_wait(barrier, 4 + 15 + 2 + jnp.where(has_cross, 3, 0).astype(jnp.int32))

    def remote(name, src, dst, device):
        k = SEMS[name]
        return pltpu.make_async_remote_copy(
            src_ref=src, dst_ref=dst, send_sem=ssem.at[k], recv_sem=rsem.at[k], device_id=device, device_id_type=MESH
        )

    sends = {}

    def leaf_send(which, rho, col, dst_rho, dst_col, device):
        sends[LOSS, which] = remote((LOSS, which), loss_h.at[leaf(rho, col)], ext.at[4 * dst_rho + dst_col], device)
        sends[PLACE, which] = remote((PLACE, which), place_h.at[leaf(rho, col)], pext.at[4 * dst_rho + dst_col], device)

    for rho in (1, 2):
        leaf_send((LONP1, LONP2)[rho - 1], rho, 2, rho, 0, (lat, at_lon(1)))
        leaf_send((LONM1, LONM2)[rho - 1], rho, 1, rho, 3, (lat, at_lon(-1)))
    for b in (0, 1):
        leaf_send((PART0, PART1)[b], 2, 1 + b, 3, 1 + b, (partner, lon))
        leaf_send((CROSS0, CROSS1)[b], 1, 1 + b, 0, 1 + b, (cross, lon))
    leaf_send(XCP, 1, 2, 0, 0, (cross, at_lon(1)))
    leaf_send(XCM, 1, 1, 0, 3, (cross, at_lon(-1)))
    for k, col in ((0, 0), (1, 3)):
        for kind, ref in ((LOSS, ext), (PLACE, pext)):
            sends[kind, (FWD0, FWD1)[k]] = remote((kind, (FWD0, FWD1)[k]), ref.at[4 * 2 + col], ref.at[4 * 3 + col], (partner, lon))
    sends[LOSS, RELP] = remote((LOSS, RELP), ext.at[0], ext.at[4], (cross, lon))
    sends[LOSS, RELM] = remote((LOSS, RELM), ext.at[1], ext.at[7], (cross, at_lon(-1)))
    sends[COEF, RELP] = remote((COEF, RELP), coef.at[0], coef.at[3], (cross, lon))
    sends[COEF, RELM] = remote((COEF, RELM), coef.at[1], coef.at[5], (cross, at_lon(-1)))
    own = coef.at[4]
    sends[COEF, LONP] = remote((COEF, LONP), own, coef.at[3], (lat, at_lon(1)))
    sends[COEF, LONM] = remote((COEF, LONM), own, coef.at[5], (lat, at_lon(-1)))
    sends[COEF, PART] = remote((COEF, PART), own, coef.at[7], (partner, lon))
    sends[COEF, CROSS] = remote((COEF, CROSS), own, coef.at[1], (cross, lon))
    sends[COEF, XCP] = remote((COEF, XCP), own, coef.at[0], (cross, at_lon(1)))
    sends[COEF, XCM] = remote((COEF, XCM), own, coef.at[2], (cross, at_lon(-1)))
    sends[COEF, FWD0] = remote((COEF, FWD0), coef.at[3], coef.at[6], (partner, lon))
    sends[COEF, FWD1] = remote((COEF, FWD1), coef.at[5], coef.at[8], (partner, lon))
    for i, j in COLUMN:
        mine = cellw.at[1, hi, lat]
        sends[CELL, (i, j)] = remote((CELL, (i, j)), mine, mine, (lax.rem(lat + i, 4), lon + j * flip))
        theirs = cellw.at[1, lax.rem(hi + j, 2), lax.rem(lat + i, 4)]
        sends[CELLF, (i, j)] = remote((CELLF, (i, j)), theirs, theirs, (partner, lon))
    sends[CELL, PART] = remote((CELL, PART), cellw.at[1, hi, lat], cellw.at[1, hi, lat], (partner, lon))
    sends[WIN, 0] = remote((WIN, 0), cellw.at[1], cellw.at[2 * par], (lat, at_lon(2 * sign)))
    sends[WINF, 0] = remote((WINF, 0), cellw.at[2 * par], cellw.at[2 * par], (partner, lon))
    for m in FAR:
        sends[GROUP, m] = remote((GROUP, m), group, gall.at[m - 2], (lat, at_lon(2 * m)))
    sends[SUM, 0] = remote((SUM, 0), part.at[0], part.at[1], (partner, lon))

    def start(*names):
        for name in names:
            sends[name].start()

    def both(*whiches):
        return [(kind, which) for which in whiches for kind in (PLACE, LOSS)]

    def only(kind, *whiches):
        return [(kind, which) for which in whiches]

    def recv(*names):
        for name in names:
            sends[name].wait_recv()

    start(*only(PLACE, LONP2, LONM2, PART0, PART1, LONP1, LONM1))
    start(*only(LOSS, PART0, PART1, LONP2, LONM2))

    @pl.when(has_cross)
    def _():
        start(*only(PLACE, CROSS0, CROSS1, XCP, XCM))

    copies[BASIS].wait()
    for k, (rho, col) in enumerate(own_slots):
        copies[k].wait()
        l = leaf(rho, col)
        coef[4, l] = mm3(basis[l], ext[4 * rho + col])
    copies[LTRANS].wait()
    cellw[1, hi, lat] = mm3(ltrans[...].reshape(256, 64), coef[4].reshape(256, 256), ((0,), (0,)))
    start((CELL, PART), *[(CELL, pair) for pair in COLUMN])
    start((COEF, PART))

    @pl.when(has_cross)
    def _():
        start((COEF, XCP), (COEF, CROSS), (COEF, XCM))
        start(*only(LOSS, XCP, CROSS0, CROSS1, XCM))

    @pl.when(jnp.logical_not(has_cross))
    def _():
        start((COEF, LONP), (COEF, LONM))
        for k in range(3):
            coef[k] = jnp.zeros((4, 64, 256), f32)

    @pl.when(jnp.logical_not(has_cross) & (hi == 0))
    def _():
        start((LOSS, LONP1))

    @pl.when(jnp.logical_not(has_cross) & (hi == 1))
    def _():
        start((LOSS, LONM1))

    for c in place_copies:
        c.wait()

    for rho, col in own_slots:
        for axis in range(2):
            row = pext[4 * rho + col, axis : axis + 1, :] * UNIT
            columns[leaf(rho, col), axis] = jnp.transpose(jnp.broadcast_to(row, (128, 512)))

    def near_source(slot):
        def body(c, carry):
            rows = pl.ds(pl.multiple_of(c * 64, 64), 64)
            high, low = split(ext[slot, rows, :])
            sh[slot, rows, :] = high
            sl[slot, rows, :] = low
            return carry

        lax.fori_loop(0, 8, body, 0)

    def near_kernel(pair, half, high_ref, low_ref):
        rho_s, col_s, rho_t, col_t = pair
        di = (rho_s - rho_t) * sign
        dj = col_s - col_t
        l = leaf(rho_t, col_t)
        slot = 4 * rho_s + col_s
        off = (1 - flags[l // 2, l % 2, 3 * (di + 1) + dj + 1]).astype(f32) * AWAY
        src_row = (pext[slot, 0:1, :] + di.astype(f32)) * UNIT + off
        src_col = (pext[slot, 1:2, :] + dj.astype(f32)) * UNIT
        for c in range(4):
            rows = slice(64 * c, 64 * c + 64)
            for j in range(4):
                lanes = slice(128 * j, 128 * j + 128)
                dr = columns[l, 0, 256 * half + 64 * c : 256 * half + 64 * c + 64, :] - src_row[:, lanes]
                dc = columns[l, 1, 256 * half + 64 * c : 256 * half + 64 * c + 64, :] - src_col[:, lanes]
                sq = dr * dr + dc * dc
                d = sq * lax.rsqrt(jnp.maximum(sq, 1e-30))
                k = (1.0 + d) * jnp.exp2(d * -LOG2E)
                high, low = split(k)
                high_ref[rows, lanes] = high
                low_ref[rows, lanes] = low

    def near_product(pair, half, high_ref, low_ref):
        rho_s, col_s, rho_t, col_t = pair
        l = leaf(rho_t, col_t)
        slot = 4 * rho_s + col_s
        high = high_ref[...]
        source = sh[slot]
        acc[l, 256 * half : 256 * half + 256, :] += mm(high, source) + mm(low_ref[...], source) + mm(high, sl[slot])

    def near(count, pair_of):
        def typed(i):
            return tuple(jnp.asarray(v, jnp.int32) for v in pair_of(i))

        near_kernel(typed(jnp.int32(0)), 0, ka_h, ka_l)

        def body(i, carry):
            pair = typed(i)
            near_kernel(pair, 1, kb_h, kb_l)
            near_product(pair, 0, ka_h, ka_l)
            near_kernel(typed(jnp.minimum(i + 1, count - 1)), 0, ka_h, ka_l)
            near_product(pair, 1, kb_h, kb_l)
            return carry

        lax.fori_loop(0, count, body, 0)

    def split_all(*slots):
        for slot in slots:
            near_source(slot)

    for k, (rho, col) in enumerate(own_slots):
        acc[leaf(rho, col)] = 0.5 * ext[4 * rho + col]
    split_all(5, 6, 9, 10)
    near(16, lambda i: (1 + i // 8, 1 + (i // 4) % 2, 1 + (i // 2) % 2, 1 + i % 2))
    recv(*[(CELL, pair) for pair in COLUMN])
    start(*[(CELLF, pair) for pair in COLUMN])
    recv(*both(PART0, PART1))
    split_all(13, 14)
    near(4, lambda i: (3, 1 + i // 2, 2, 1 + i % 2))

    copies[DTRANS].wait()
    recv((CELL, PART), *[(CELLF, pair) for pair in COLUMN])
    start((WIN, 0))
    first = 2 * par
    total = jnp.zeros((64, 256), f32)
    for f in range(2):
        for e in range(2):
            total += mm3(dtrans[first + e, f], cellw[1, f, first + e], ((0,), (0,)))
    group[...] = total
    start(*[(GROUP, m) for m in FAR])

    @pl.when(jnp.logical_not(has_cross) & (hi == 0))
    def _():
        start((LOSS, LONM1))

    @pl.when(jnp.logical_not(has_cross) & (hi == 1))
    def _():
        start((LOSS, LONP1))

    @pl.when(has_cross)
    def _():
        recv((COEF, XCP), (COEF, CROSS))
        start((COEF, RELP), (COEF, RELM))

    recv(*both(LONP2, LONM2))
    start(*both(FWD0, FWD1))
    split_all(8, 11)
    near(4, lambda i: (2, 3 * (i // 2), 1 + i % 2, 1 + i // 2))

    @pl.when(has_cross)
    def _():
        recv(*both(XCP, CROSS0))
        start((LOSS, RELP), (LOSS, RELM))
        recv(*both(CROSS1, XCM), (COEF, RELP), (COEF, RELM))

    @pl.when(jnp.logical_not(has_cross))
    def _():
        recv((COEF, LONP), (COEF, LONM))

    start((COEF, FWD0), (COEF, FWD1))
    recv((WIN, 0))
    start((WINF, 0))

    @pl.when(has_cross)
    def _():
        split_all(0, 1, 2, 3)
        near(6, lambda i: (0, (i + 1) // 2, 1, jnp.where(i % 2 == 1, jnp.maximum(1, (i - 1) // 2), jnp.minimum(2, i // 2 + 1))))

    recv(*both(FWD0, FWD1))
    split_all(12, 15)
    near(2, lambda i: (3, 3 * i, 2, 1 + i))

    copies[DCOUP].wait()
    copies[GCOUP].wait()
    copies[LCOUP].wait()
    recv((COEF, PART), (COEF, FWD0), (COEF, FWD1))

    @pl.when(has_cross)
    def _():
        recv((COEF, XCM))

    field[...] = jnp.zeros((256, 256), f32)

    def leaf_body(i, carry):
        side, v_side = i // 3, i % 3
        slot = 3 * (side + par * (2 - 2 * side)) + v_side
        total = field[...]
        for a in range(2):
            for b in range(2):
                u, v = 2 * side + a, 2 * v_side + b
                w = 6 * u + v
                weights = []
                for l in range(4):
                    di, dj = u - 2 - l // 2, v - 2 - l % 2
                    inside = (jnp.abs(di) <= 1) & (jnp.abs(dj) <= 1)
                    index = 3 * (jnp.clip(di, -1, 1) + 1) + jnp.clip(dj, -1, 1) + 1
                    keep = (1 - flags[l // 2, l % 2, index] * jnp.where(inside, 1, 0)).astype(f32)
                    weights.append((lcoup[l, w].astype(f32) * keep).astype(bf16))
                total += mm2(jnp.concatenate(weights, 0), coef[slot, 2 * a + b])
        field[...] = total
        return carry

    lax.fori_loop(0, 9, leaf_body, 0)

    def last(side, t):
        return (jnp.int32(1), jnp.int32(3 * side), jnp.asarray(1 + t, jnp.int32), jnp.int32(1 + side))

    def halves(side, t, fn):
        for half in range(2):
            rows = pl.ds(256 * half, 256)
            fn(last(side, t), half, kw_h.at[2 * side + t, rows], kw_l.at[2 * side + t, rows])

    recv(*only(PLACE, LONP1, LONM1))
    for side in range(2):

        def prepare(t, carry, side=side):
            halves(side, t, near_kernel)
            return carry

        lax.fori_loop(0, 2, prepare, 0)

    recv((WINF, 0))

    def window_body(v, total):
        hoff, f = v // 2, v % 2
        for row in range(4):
            w = 6 * (row + 2 - 2 * row_group) + v
            away = (jnp.abs(row - lat) > 1) | (jnp.abs(v - 2 - hi) > 1)
            keep = jnp.where(away, 1.0, 0.0)
            weight = (dcoup[w].astype(f32) * keep).astype(bf16)
            total += mm2(weight, cellw[hoff, f, row])
        return total

    device_far = lax.fori_loop(0, 6, window_body, jnp.zeros((64, 256), f32))
    recv(*[(GROUP, m) for m in FAR])
    total = jnp.zeros((64, 256), f32)
    for m in FAR:
        total += mm2(gcoup[lax.rem(col_group - m + 16, 16)], gall[m - 2])
    part[0] = total
    start((SUM, 0))
    recv((SUM, 0))
    device_field = device_far + mm3(dtrans[lat, hi], part[0] + part[1])
    field[...] += mm3(ltrans[...].reshape(256, 64), device_field)
    for l in range(4):
        acc[l] += mm3(basis[l], field[pl.ds(64 * l, 64), :], ((0,), (0,)))

    for side, straight, relayed in ((0, LONP1, RELP), (1, LONM1, RELM)):

        @pl.when(jnp.logical_not(has_cross))
        def _():
            recv((LOSS, straight))

        @pl.when(has_cross)
        def _():
            recv((LOSS, relayed))

        split_all(4 + 3 * side)

        def finish(t, carry, side=side):
            halves(side, t, near_product)
            return carry

        lax.fori_loop(0, 2, finish, 0)

    crossing = [(COEF, w) for w in (CROSS, XCP, XCM, RELP, RELM)] + both(CROSS0, CROSS1, XCP, XCM)
    crossing += only(LOSS, RELP, RELM)
    direct = [(COEF, LONP), (COEF, LONM)] + only(LOSS, LONP1, LONM1)
    for name in sends:
        if name not in crossing and name not in direct:
            sends[name].wait_send()

    @pl.when(has_cross)
    def _():
        for name in crossing:
            sends[name].wait_send()

    @pl.when(jnp.logical_not(has_cross))
    def _():
        for name in direct:
            sends[name].wait_send()


def local(losses, positions, leaf_basis, near_flags, leaf_coupling, leaf_transfer, device_coupling, device_transfer, group_coupling):
    anywhere = pl.BlockSpec(memory_space=pl.ANY)
    vmem = pltpu.VMEM
    call = pl.pallas_call(
        kernel,
        out_shape=jax.ShapeDtypeStruct((4, 512, 256), f32),
        in_specs=[anywhere, anywhere, pl.BlockSpec(memory_space=pltpu.SMEM)] + [anywhere] * 6,
        out_specs=pl.BlockSpec(memory_space=pltpu.VMEM),
        scratch_shapes=[
            vmem((16, 512, 256), f32), vmem((16, 2, 512), f32), vmem((9, 4, 64, 256), f32),
            vmem((3, 2, 4, 64, 256), f32), vmem((64, 256), f32), vmem((13, 64, 256), f32), vmem((2, 64, 256), f32),
            vmem((256, 512), bf16), vmem((256, 512), bf16),
            vmem((256, 512), bf16), vmem((256, 512), bf16),
            vmem((16, 512, 256), bf16), vmem((16, 512, 256), bf16), vmem((256, 256), f32), vmem((4, 2, 512, 128), f32),
            vmem((4, 512, 512), bf16), vmem((4, 512, 512), bf16),
            vmem((4, 64, 512), f32), vmem((4, 36, 64, 64), bf16), vmem((4, 64, 64), f32),
            vmem((36, 64, 64), bf16), vmem((4, 2, 64, 64), f32), vmem((16, 64, 64), bf16),
            pltpu.SemaphoreType.DMA((14,)),
            pltpu.SemaphoreType.DMA((len(SEMS),)), pltpu.SemaphoreType.DMA((len(SEMS),)),
        ],
        compiler_params=pltpu.CompilerParams(collective_id=0, has_side_effects=True, vmem_limit_bytes=40 * 1024 * 1024),
        name="apply",
    )
    hbm = lambda x: pltpu.with_memory_space_constraint(x, pltpu.HBM)
    out = call(
        hbm(losses.reshape(4, 512, 256)), hbm(positions.reshape(4, 2, 512)), near_flags,
        hbm(jnp.swapaxes(leaf_basis, 2, 3).reshape(4, 64, 512)), hbm(leaf_coupling.reshape(4, 36, 64, 64)),
        hbm(leaf_transfer.reshape(4, 64, 64)), hbm(device_coupling.reshape(36, 64, 64)), hbm(device_transfer), hbm(group_coupling),
    )
    return out.reshape(2, 2, 512, 256)


def solution(mesh):
    placed = (
        P("lat", "lon", None, None),
        P("lat", "lon", None, None),
        P("lat", "lon", None, None),
        P("lat", "lon", None),
        P("lat", "lon", None, None, None),
        P("lat", "lon", None, None),
        P("lat", "lon", None, None, None),
        P(),
        P(),
    )
    return jax.shard_map(
        local, mesh=mesh, in_specs=placed, out_specs=P("lat", "lon", None, None), check_vma=False
    )
```

```python
import jax
import jax.numpy as jnp
from jax import lax
from jax.experimental import pallas as pl
from jax.experimental.pallas import tpu as pltpu
from jax.sharding import PartitionSpec as P

MESH = pl.DeviceIdType.MESH
LOG2E = 1.4426950408889634
UNIT = 1.7320508075688772 / 0.15
AWAY = 1.0e4
f32, bf16 = jnp.float32, jnp.bfloat16


LOSS, PLACE, COEF, CELL, CELLF, WIN, WINF, GROUP, SUM = range(9)
LONP, LONM, LONP1, LONP2, LONM1, LONM2, PART, PART0, PART1, CROSS, CROSS0, CROSS1, XCP, XCM, FWD0, FWD1, RELP, RELM = range(18)
BASIS, LCOUP, LTRANS, DCOUP, DTRANS, GCOUP = range(10, 16)


def split(x):
    high = x.astype(bf16)
    return high, (x - high.astype(f32)).astype(bf16)


def mm(a, b, dims=((1,), (0,))):
    return lax.dot_general(a, b, (dims, ((), ())), preferred_element_type=f32)


def mm3(a, b, dims=((1,), (0,))):
    ah, al = split(a)
    bh, bl = split(b)
    return mm(ah, bh, dims) + mm(al, bh, dims) + mm(ah, bl, dims)


def mm2(a, b):
    bh, bl = split(b)
    return mm(a, bh) + mm(a, bl)


FAR = tuple(range(2, 15))
COLUMN = ((2, 0), (0, 1), (2, 1))


def remote_names():
    names = []
    for kind in (LOSS, PLACE):
        for which in (LONP1, LONP2, LONM1, LONM2, PART0, PART1, CROSS0, CROSS1, XCP, XCM, FWD0, FWD1, RELP, RELM):
            names.append((kind, which))
    for which in (LONP, LONM, PART, CROSS, XCP, XCM, FWD0, FWD1, RELP, RELM):
        names.append((COEF, which))
    for pair in COLUMN:
        names += [(CELL, pair), (CELLF, pair)]
    names += [(CELL, PART), (WIN, 0), (WINF, 0), (SUM, 0)]
    for m in FAR:
        names.append((GROUP, m))
    return {name: k for k, name in enumerate(names)}


SEMS = remote_names()


def kernel(
    loss_h, place_h, flags, basis_h, lcoup_h, ltrans_h, dcoup_h, dtrans_h, gcoup_h,
    acc,
    ext, pext, coef, cellw, group, gall, part, ka_h, ka_l, kb_h, kb_l, sh, sl, field, columns, kw_h, kw_l,
    basis, lcoup, ltrans, dcoup, dtrans, gcoup,
    lsem, ssem, rsem,
):
    lat, lon = lax.axis_index("lat"), lax.axis_index("lon")
    n_lon = lax.axis_size("lon")
    par, hi = lax.rem(lat, 2), lax.rem(lon, 2)
    row_group, col_group = lat // 2, lon // 2
    sign = 1 - 2 * par
    has_cross = (lat == 1) | (lat == 2)
    partner, cross = lat + sign, lat - sign

    def leaf(rho, col):
        return 2 * (par + (rho - 1) * sign) + (col - 1)

    def at_lon(step):
        return lax.rem(lon + step + n_lon, n_lon)

    def local(src, dst, k):
        return pltpu.make_async_copy(src, dst, lsem.at[k])

    own_slots = [(1, 1), (1, 2), (2, 1), (2, 2)]
    copies = {}
    for k, (rho, col) in enumerate(own_slots):
        copies[k] = local(loss_h.at[leaf(rho, col)], ext.at[4 * rho + col], k)
    for k, (src, dst, name) in enumerate((
        (basis_h, basis, BASIS), (lcoup_h, lcoup, LCOUP), (ltrans_h, ltrans, LTRANS),
        (dcoup_h, dcoup, DCOUP), (dtrans_h.at[:, pl.ds(2 * col_group, 2)], dtrans, DTRANS),
        (gcoup_h.at[row_group, col_group, par], gcoup, GCOUP),
    )):
        copies[name] = local(src, dst, 4 + k)
    place_copies = [
        local(place_h.at[leaf(rho, col)], pext.at[4 * rho + col], 10 + k) for k, (rho, col) in enumerate(own_slots)
    ]
    for k in range(4):
        copies[k].start()
    for name in (BASIS, LTRANS):
        copies[name].start()
    for c in place_copies:
        c.start()
    for name in (DTRANS, LCOUP, DCOUP, GCOUP):
        copies[name].start()

    barrier = pltpu.get_barrier_semaphore()

    def hello(a, b):
        pl.semaphore_signal(barrier, inc=1, device_id=(a, b), device_id_type=MESH)

    flip = 1 - 2 * hi
    for i, j in COLUMN:
        hello(lax.rem(lat + i, 4), lon + j * flip)
    hello(partner, lon)
    for m in range(1, 16):
        hello(lat, at_lon(2 * m))
    hello(lat, at_lon(1))
    hello(lat, at_lon(-1))

    @pl.when(has_cross)
    def _():
        hello(cross, lon)
        hello(cross, at_lon(1))
        hello(cross, at_lon(-1))

    pl.semaphore_wait(barrier, 4 + 15 + 2 + jnp.where(has_cross, 3, 0).astype(jnp.int32))

    def remote(name, src, dst, device):
        k = SEMS[name]
        return pltpu.make_async_remote_copy(
            src_ref=src, dst_ref=dst, send_sem=ssem.at[k], recv_sem=rsem.at[k], device_id=device, device_id_type=MESH
        )

    sends = {}

    def leaf_send(which, rho, col, dst_rho, dst_col, device):
        sends[LOSS, which] = remote((LOSS, which), loss_h.at[leaf(rho, col)], ext.at[4 * dst_rho + dst_col], device)
        sends[PLACE, which] = remote((PLACE, which), place_h.at[leaf(rho, col)], pext.at[4 * dst_rho + dst_col], device)

    for rho in (1, 2):
        leaf_send((LONP1, LONP2)[rho - 1], rho, 2, rho, 0, (lat, at_lon(1)))
        leaf_send((LONM1, LONM2)[rho - 1], rho, 1, rho, 3, (lat, at_lon(-1)))
    for b in (0, 1):
        leaf_send((PART0, PART1)[b], 2, 1 + b, 3, 1 + b, (partner, lon))
        leaf_send((CROSS0, CROSS1)[b], 1, 1 + b, 0, 1 + b, (cross, lon))
    leaf_send(XCP, 1, 2, 0, 0, (cross, at_lon(1)))
    leaf_send(XCM, 1, 1, 0, 3, (cross, at_lon(-1)))
    for k, col in ((0, 0), (1, 3)):
        for kind, ref in ((LOSS, ext), (PLACE, pext)):
            sends[kind, (FWD0, FWD1)[k]] = remote((kind, (FWD0, FWD1)[k]), ref.at[4 * 2 + col], ref.at[4 * 3 + col], (partner, lon))
    sends[LOSS, RELP] = remote((LOSS, RELP), ext.at[0], ext.at[4], (cross, lon))
    sends[LOSS, RELM] = remote((LOSS, RELM), ext.at[1], ext.at[7], (cross, at_lon(-1)))
    sends[COEF, RELP] = remote((COEF, RELP), coef.at[0], coef.at[3], (cross, lon))
    sends[COEF, RELM] = remote((COEF, RELM), coef.at[1], coef.at[5], (cross, at_lon(-1)))
    own = coef.at[4]
    sends[COEF, LONP] = remote((COEF, LONP), own, coef.at[3], (lat, at_lon(1)))
    sends[COEF, LONM] = remote((COEF, LONM), own, coef.at[5], (lat, at_lon(-1)))
    sends[COEF, PART] = remote((COEF, PART), own, coef.at[7], (partner, lon))
    sends[COEF, CROSS] = remote((COEF, CROSS), own, coef.at[1], (cross, lon))
    sends[COEF, XCP] = remote((COEF, XCP), own, coef.at[0], (cross, at_lon(1)))
    sends[COEF, XCM] = remote((COEF, XCM), own, coef.at[2], (cross, at_lon(-1)))
    sends[COEF, FWD0] = remote((COEF, FWD0), coef.at[3], coef.at[6], (partner, lon))
    sends[COEF, FWD1] = remote((COEF, FWD1), coef.at[5], coef.at[8], (partner, lon))
    for i, j in COLUMN:
        mine = cellw.at[1, hi, lat]
        sends[CELL, (i, j)] = remote((CELL, (i, j)), mine, mine, (lax.rem(lat + i, 4), lon + j * flip))
        theirs = cellw.at[1, lax.rem(hi + j, 2), lax.rem(lat + i, 4)]
        sends[CELLF, (i, j)] = remote((CELLF, (i, j)), theirs, theirs, (partner, lon))
    sends[CELL, PART] = remote((CELL, PART), cellw.at[1, hi, lat], cellw.at[1, hi, lat], (partner, lon))
    sends[WIN, 0] = remote((WIN, 0), cellw.at[1], cellw.at[2 * par], (lat, at_lon(2 * sign)))
    sends[WINF, 0] = remote((WINF, 0), cellw.at[2 * par], cellw.at[2 * par], (partner, lon))
    for m in FAR:
        sends[GROUP, m] = remote((GROUP, m), group, gall.at[m - 2], (lat, at_lon(2 * m)))
    sends[SUM, 0] = remote((SUM, 0), part.at[0], part.at[1], (partner, lon))

    def start(*names):
        for name in names:
            sends[name].start()

    def both(*whiches):
        return [(kind, which) for which in whiches for kind in (PLACE, LOSS)]

    def only(kind, *whiches):
        return [(kind, which) for which in whiches]

    def recv(*names):
        for name in names:
            sends[name].wait_recv()

    start(*only(PLACE, LONP2, LONM2, PART0, PART1, LONP1, LONM1))
    start(*only(LOSS, PART0, PART1, LONP2, LONM2))

    @pl.when(has_cross)
    def _():
        start(*only(PLACE, CROSS0, CROSS1, XCP, XCM))

    copies[BASIS].wait()
    for k, (rho, col) in enumerate(own_slots):
        copies[k].wait()
        l = leaf(rho, col)
        coef[4, l] = mm3(basis[l], ext[4 * rho + col])
    copies[LTRANS].wait()
    cellw[1, hi, lat] = mm3(ltrans[...].reshape(256, 64), coef[4].reshape(256, 256), ((0,), (0,)))
    start((CELL, PART), *[(CELL, pair) for pair in COLUMN])
    start((COEF, PART))

    @pl.when(has_cross)
    def _():
        start((COEF, XCP), (COEF, CROSS), (COEF, XCM))
        start(*only(LOSS, XCP, CROSS0, CROSS1, XCM))

    @pl.when(jnp.logical_not(has_cross))
    def _():
        start((COEF, LONP), (COEF, LONM))
        for k in range(3):
            coef[k] = jnp.zeros((4, 64, 256), f32)

    @pl.when(jnp.logical_not(has_cross) & (hi == 0))
    def _():
        start((LOSS, LONP1))

    @pl.when(jnp.logical_not(has_cross) & (hi == 1))
    def _():
        start((LOSS, LONM1))

    for c in place_copies:
        c.wait()

    for rho, col in own_slots:
        for axis in range(2):
            row = pext[4 * rho + col, axis : axis + 1, :] * UNIT
            columns[leaf(rho, col), axis] = jnp.transpose(jnp.broadcast_to(row, (128, 512)))

    def near_source(slot):
        def body(c, carry):
            rows = pl.ds(pl.multiple_of(c * 64, 64), 64)
            high, low = split(ext[slot, rows, :])
            sh[slot, rows, :] = high
            sl[slot, rows, :] = low
            return carry

        lax.fori_loop(0, 8, body, 0)

    def near_kernel(pair, half, high_ref, low_ref):
        rho_s, col_s, rho_t, col_t = pair
        di = (rho_s - rho_t) * sign
        dj = col_s - col_t
        l = leaf(rho_t, col_t)
        slot = 4 * rho_s + col_s
        off = (1 - flags[l // 2, l % 2, 3 * (di + 1) + dj + 1]).astype(f32) * AWAY
        src_row = (pext[slot, 0:1, :] + di.astype(f32)) * UNIT + off
        src_col = (pext[slot, 1:2, :] + dj.astype(f32)) * UNIT
        for c in range(4):
            rows = slice(64 * c, 64 * c + 64)
            for j in range(4):
                lanes = slice(128 * j, 128 * j + 128)
                dr = columns[l, 0, 256 * half + 64 * c : 256 * half + 64 * c + 64, :] - src_row[:, lanes]
                dc = columns[l, 1, 256 * half + 64 * c : 256 * half + 64 * c + 64, :] - src_col[:, lanes]
                sq = dr * dr + dc * dc
                d = sq * lax.rsqrt(jnp.maximum(sq, 1e-30))
                k = (1.0 + d) * jnp.exp2(d * -LOG2E)
                high, low = split(k)
                high_ref[rows, lanes] = high
                low_ref[rows, lanes] = low

    def near_product(pair, half, high_ref, low_ref):
        rho_s, col_s, rho_t, col_t = pair
        l = leaf(rho_t, col_t)
        slot = 4 * rho_s + col_s
        high = high_ref[...]
        source = sh[slot]
        acc[l, 256 * half : 256 * half + 256, :] += mm(high, source) + mm(low_ref[...], source) + mm(high, sl[slot])

    def near(count, pair_of):
        def typed(i):
            return tuple(jnp.asarray(v, jnp.int32) for v in pair_of(i))

        near_kernel(typed(jnp.int32(0)), 0, ka_h, ka_l)

        def body(i, carry):
            pair = typed(i)
            near_kernel(pair, 1, kb_h, kb_l)
            near_product(pair, 0, ka_h, ka_l)
            near_kernel(typed(jnp.minimum(i + 1, count - 1)), 0, ka_h, ka_l)
            near_product(pair, 1, kb_h, kb_l)
            return carry

        lax.fori_loop(0, count, body, 0)

    def split_all(*slots):
        for slot in slots:
            near_source(slot)

    for k, (rho, col) in enumerate(own_slots):
        acc[leaf(rho, col)] = 0.5 * ext[4 * rho + col]
    split_all(5, 6, 9, 10)
    own_pair = lambda i: (1 + i // 8, 1 + (i // 4) % 2, 1 + (i // 2) % 2, 1 + i % 2)
    near(8, own_pair)
    recv(*both(PART0, PART1))
    split_all(13, 14)
    near(4, lambda i: (3, 1 + i // 2, 2, 1 + i % 2))
    recv(*[(CELL, pair) for pair in COLUMN])
    start(*[(CELLF, pair) for pair in COLUMN])
    near(2, lambda i: own_pair(i + 8))

    copies[DTRANS].wait()
    recv((CELL, PART), *[(CELLF, pair) for pair in COLUMN])
    start((WIN, 0))
    first = 2 * par
    total = jnp.zeros((64, 256), f32)
    for f in range(2):
        for e in range(2):
            total += mm3(dtrans[first + e, f], cellw[1, f, first + e], ((0,), (0,)))
    group[...] = total
    start(*[(GROUP, m) for m in FAR])

    @pl.when(jnp.logical_not(has_cross) & (hi == 0))
    def _():
        start((LOSS, LONM1))

    @pl.when(jnp.logical_not(has_cross) & (hi == 1))
    def _():
        start((LOSS, LONP1))

    near(6, lambda i: own_pair(i + 10))

    @pl.when(has_cross)
    def _():
        recv((COEF, XCP), (COEF, CROSS))
        start((COEF, RELP), (COEF, RELM))

    recv(*both(LONP2, LONM2))
    start(*both(FWD0, FWD1))
    split_all(8, 11)
    near(4, lambda i: (2, 3 * (i // 2), 1 + i % 2, 1 + i // 2))

    @pl.when(has_cross)
    def _():
        recv(*both(XCP, CROSS0))
        start((LOSS, RELP), (LOSS, RELM))
        recv(*both(CROSS1, XCM), (COEF, RELP), (COEF, RELM))

    @pl.when(jnp.logical_not(has_cross))
    def _():
        recv((COEF, LONP), (COEF, LONM))

    start((COEF, FWD0), (COEF, FWD1))
    recv((WIN, 0))
    start((WINF, 0))

    @pl.when(has_cross)
    def _():
        split_all(0, 1, 2, 3)
        near(6, lambda i: (0, (i + 1) // 2, 1, jnp.where(i % 2 == 1, jnp.maximum(1, (i - 1) // 2), jnp.minimum(2, i // 2 + 1))))

    recv(*both(FWD0, FWD1))
    split_all(12, 15)
    near(2, lambda i: (3, 3 * i, 2, 1 + i))

    copies[DCOUP].wait()
    copies[GCOUP].wait()
    copies[LCOUP].wait()
    recv((COEF, PART), (COEF, FWD0), (COEF, FWD1))

    @pl.when(has_cross)
    def _():
        recv((COEF, XCM))

    field[...] = jnp.zeros((256, 256), f32)

    def leaf_body(i, carry):
        side, v_side = i // 3, i % 3
        slot = 3 * (side + par * (2 - 2 * side)) + v_side
        total = field[...]
        for a in range(2):
            for b in range(2):
                u, v = 2 * side + a, 2 * v_side + b
                w = 6 * u + v
                weights = []
                for l in range(4):
                    di, dj = u - 2 - l // 2, v - 2 - l % 2
                    inside = (jnp.abs(di) <= 1) & (jnp.abs(dj) <= 1)
                    index = 3 * (jnp.clip(di, -1, 1) + 1) + jnp.clip(dj, -1, 1) + 1
                    keep = (1 - flags[l // 2, l % 2, index] * jnp.where(inside, 1, 0)).astype(f32)
                    weights.append((lcoup[l, w].astype(f32) * keep).astype(bf16))
                total += mm2(jnp.concatenate(weights, 0), coef[slot, 2 * a + b])
        field[...] = total
        return carry

    lax.fori_loop(0, 9, leaf_body, 0)

    def last(side, t):
        return (jnp.int32(1), jnp.int32(3 * side), jnp.asarray(1 + t, jnp.int32), jnp.int32(1 + side))

    def halves(side, t, fn):
        for half in range(2):
            rows = pl.ds(256 * half, 256)
            fn(last(side, t), half, kw_h.at[2 * side + t, rows], kw_l.at[2 * side + t, rows])

    recv(*only(PLACE, LONP1, LONM1))
    for side in range(2):

        def prepare(t, carry, side=side):
            halves(side, t, near_kernel)
            return carry

        lax.fori_loop(0, 2, prepare, 0)

    recv((WINF, 0))

    def window_body(v, total):
        hoff, f = v // 2, v % 2
        for row in range(4):
            w = 6 * (row + 2 - 2 * row_group) + v
            away = (jnp.abs(row - lat) > 1) | (jnp.abs(v - 2 - hi) > 1)
            keep = jnp.where(away, 1.0, 0.0)
            weight = (dcoup[w].astype(f32) * keep).astype(bf16)
            total += mm2(weight, cellw[hoff, f, row])
        return total

    device_far = lax.fori_loop(0, 6, window_body, jnp.zeros((64, 256), f32))
    recv(*[(GROUP, m) for m in FAR])
    total = jnp.zeros((64, 256), f32)
    for m in FAR:
        total += mm2(gcoup[lax.rem(col_group - m + 16, 16)], gall[m - 2])
    part[0] = total
    start((SUM, 0))
    recv((SUM, 0))
    device_field = device_far + mm3(dtrans[lat, hi], part[0] + part[1])
    field[...] += mm3(ltrans[...].reshape(256, 64), device_field)
    for l in range(4):
        acc[l] += mm3(basis[l], field[pl.ds(64 * l, 64), :], ((0,), (0,)))

    for side, straight, relayed in ((0, LONP1, RELP), (1, LONM1, RELM)):

        @pl.when(jnp.logical_not(has_cross))
        def _():
            recv((LOSS, straight))

        @pl.when(has_cross)
        def _():
            recv((LOSS, relayed))

        split_all(4 + 3 * side)

        def finish(t, carry, side=side):
            halves(side, t, near_product)
            return carry

        lax.fori_loop(0, 2, finish, 0)

    crossing = [(COEF, w) for w in (CROSS, XCP, XCM, RELP, RELM)] + both(CROSS0, CROSS1, XCP, XCM)
    crossing += only(LOSS, RELP, RELM)
    direct = [(COEF, LONP), (COEF, LONM)] + only(LOSS, LONP1, LONM1)
    for name in sends:
        if name not in crossing and name not in direct:
            sends[name].wait_send()

    @pl.when(has_cross)
    def _():
        for name in crossing:
            sends[name].wait_send()

    @pl.when(jnp.logical_not(has_cross))
    def _():
        for name in direct:
            sends[name].wait_send()


def local(losses, positions, leaf_basis, near_flags, leaf_coupling, leaf_transfer, device_coupling, device_transfer, group_coupling):
    anywhere = pl.BlockSpec(memory_space=pl.ANY)
    vmem = pltpu.VMEM
    call = pl.pallas_call(
        kernel,
        out_shape=jax.ShapeDtypeStruct((4, 512, 256), f32),
        in_specs=[anywhere, anywhere, pl.BlockSpec(memory_space=pltpu.SMEM)] + [anywhere] * 6,
        out_specs=pl.BlockSpec(memory_space=pltpu.VMEM),
        scratch_shapes=[
            vmem((16, 512, 256), f32), vmem((16, 2, 512), f32), vmem((9, 4, 64, 256), f32),
            vmem((3, 2, 4, 64, 256), f32), vmem((64, 256), f32), vmem((13, 64, 256), f32), vmem((2, 64, 256), f32),
            vmem((256, 512), bf16), vmem((256, 512), bf16),
            vmem((256, 512), bf16), vmem((256, 512), bf16),
            vmem((16, 512, 256), bf16), vmem((16, 512, 256), bf16), vmem((256, 256), f32), vmem((4, 2, 512, 128), f32),
            vmem((4, 512, 512), bf16), vmem((4, 512, 512), bf16),
            vmem((4, 64, 512), f32), vmem((4, 36, 64, 64), bf16), vmem((4, 64, 64), f32),
            vmem((36, 64, 64), bf16), vmem((4, 2, 64, 64), f32), vmem((16, 64, 64), bf16),
            pltpu.SemaphoreType.DMA((14,)),
            pltpu.SemaphoreType.DMA((len(SEMS),)), pltpu.SemaphoreType.DMA((len(SEMS),)),
        ],
        compiler_params=pltpu.CompilerParams(collective_id=0, has_side_effects=True, vmem_limit_bytes=40 * 1024 * 1024),
        name="apply",
    )
    hbm = lambda x: pltpu.with_memory_space_constraint(x, pltpu.HBM)
    out = call(
        hbm(losses.reshape(4, 512, 256)), hbm(positions.reshape(4, 2, 512)), near_flags,
        hbm(jnp.swapaxes(leaf_basis, 2, 3).reshape(4, 64, 512)), hbm(leaf_coupling.reshape(4, 36, 64, 64)),
        hbm(leaf_transfer.reshape(4, 64, 64)), hbm(device_coupling.reshape(36, 64, 64)), hbm(device_transfer), hbm(group_coupling),
    )
    return out.reshape(2, 2, 512, 256)


def solution(mesh):
    placed = (
        P("lat", "lon", None, None),
        P("lat", "lon", None, None),
        P("lat", "lon", None, None),
        P("lat", "lon", None),
        P("lat", "lon", None, None, None),
        P("lat", "lon", None, None),
        P("lat", "lon", None, None, None),
        P(),
        P(),
    )
    return jax.shard_map(
        local, mesh=mesh, in_specs=placed, out_specs=P("lat", "lon", None, None), check_vma=False
    )
```
